256 devices in a mesh: dp: 64 (over z, y, core), expert: 4 (over x).
Axes of the slice: x: 4, y: 4, z: 8, core: 2. Of those that a mesh axis runs over, the one named last changes fastest.
Arguments:
- tokens: bfloat16 [32768, 2048], P(('dp', 'expert')), may hold values from -6 to 6
- cotangent: bfloat16 [32768, 2048], P(('dp', 'expert')), may hold values from -6 to 6
- expert_ids: int32 [32768, 2], P(('dp', 'expert')), may hold values from 0 to 3, all different within a row; in each aligned block of 128 rows (0 to 127, 128 to 255, ...) at most 80 rows name the same one
- gate_probs: float32 [32768, 2], P(('dp', 'expert')), may hold values from 0.2 to 1
- gate_up_weight: bfloat16 [4, 2048, 1024], P('expert'), may hold values from -0.125 to 0.125
- down_weight: bfloat16 [4, 512, 2048], P('expert'), may hold values from -0.25 to 0.25
- down_residual: bfloat16 [64, 4, 512, 2048], P('dp', 'expert'), may hold values from -32 to 32
Outputs:
- token_grad: bfloat16 [32768, 2048], P(('dp', 'expert'))
- grad_gate_up: float32 [4, 2048, 1024], P('expert', 'dp')
- grad_down: float32 [4, 512, 2048], P('expert', 'dp')
The draws below stay inside these ranges and needn't reach their ends.
Inputs may be any that keep to these rules, and one draw needn't show every extreme that they name: `expert_ids`: each token names 2 different experts. Among the tokens of one device no expert is named by more than 80 tokens, and in some device's tokens one expert is named by exactly 80.
All inputs are finite; a program needn't handle non-finite values.
Results may differ from the reference program's by a relative error of at most 0.0065.
Values may be sent and summed in bfloat16 or wider, within the bound.
A program may use at most 128 MiB of HBM per device.

```python
import math
import jax
import jax.numpy as jnp
import numpy as np
from jax import lax

D = 2048
TOP = 2
H_DEV = 512
TOK_DEV = 128
EXPERTS = 4
DP_GROUPS = 64
CAP = 80
TOKENS = 32768


def strengthened(values, key, source, target, blocks, factor):
    owner, partner = [(jnp.arange(values.shape[position]) // (values.shape[position] // blocks)).reshape([-1 if axis == position else 1 for axis in range(values.ndim)]) for position in (source, target)]
    chosen = jax.random.permutation(key, blocks)[partner]
    strong = (owner == chosen) | (owner == (partner + blocks // 2) % blocks)
    return jnp.where(strong, factor * values, values)


def level_of(key, dims, split, low, top_value):
    factor_of, own = 1.0, jax.random.fold_in(key, 6)
    for axis_at, shards_of in split:
        draws = jnp.exp(jax.random.uniform(jax.random.fold_in(own, axis_at), (shards_of,), jnp.float32, low / len(split), top_value / len(split)))
        factor_of = factor_of * jnp.repeat(draws, dims[axis_at] // shards_of).reshape([-1 if axis == axis_at else 1 for axis in range(len(dims))])
    return factor_of


def deal_out(key, own, number, rows, count, top, reach, slope):
    ranking = jax.random.permutation(key, count)
    packed, usual = shares(count, rows * top, reach, slope, True), shares(count, rows * top, reach, slope, False)
    places = jnp.arange(count)

    def named(lengths, rotation):
        used = int((lengths > 0).sum())
        fixed = max(1, used // 4)
        moved = fixed + (places - fixed + rotation * (used - fixed)) % max(1, count - fixed)
        return jnp.zeros((count,), jnp.int32).at[ranking[jnp.where(places < fixed, places, moved)]].set(jnp.asarray(lengths, jnp.int32))

    lengths = jnp.where(number % 4 == 0, named(packed, number // 4), named(usual, number - number // 4 - 1))
    mixed = jax.random.permutation(jax.random.fold_in(own, 3), count)
    giver, receiver = mixed[0:count // 2 * 2:2], mixed[1:count // 2 * 2:2]
    margin = jnp.minimum(lengths[giver] - 1, reach - lengths[receiver]) // 2
    margin = jnp.where((giver == ranking[0]) | (receiver == ranking[0]) | (lengths[receiver] == 0), 0, jnp.maximum(margin, 0))
    moved = jax.random.randint(jax.random.fold_in(own, 4), (count // 2,), 0, 1 << 20) % (margin + 1)
    lengths = lengths.at[giver].add(-moved).at[receiver].add(moved)
    members = jnp.searchsorted(jnp.cumsum(lengths), jnp.arange(rows * top), side="right").astype(jnp.int32)
    table = members.reshape(top, rows).T
    table = table[jax.random.permutation(jax.random.fold_in(own, 1), rows)]
    rotation = jax.random.randint(jax.random.fold_in(own, 2), (rows, 1), 0, top)
    return jnp.take_along_axis(table, (jnp.arange(top)[None, :] + rotation) % top, axis=1)


def shares(number_of, total, limit, skew, full):
    weights = [(1 << 20) // math.isqrt(rank ** skew) + 1 for rank in range(1, number_of + 1)]
    largest = limit if full else min(limit, max(-(-total // number_of), total * weights[0] // sum(weights)))
    least = 1 if total - largest >= number_of - 1 else 0
    counts, rest = [largest] + [least] * (number_of - 1), total - largest - least * (number_of - 1)
    while rest > 0:
        free = [i for i in range(1, number_of) if counts[i] < largest] or [i for i in range(1, number_of) if counts[i] < limit]
        whole, remaining = sum([weights[i] for i in free]), rest
        for i in free:
            extra = min(limit - counts[i], max(1, remaining * weights[i] // whole), rest)
            counts[i] = counts[i] + extra
            rest = rest - extra
    return np.array(counts)


def noise(rng, extent, deviation, bound, cuts=(), held_as=jnp.bfloat16):
    loudness = level_of(rng, extent, cuts, -0.22, 0.18) if cuts else 1.0
    drawn = jax.random.normal(rng, extent, jnp.float32) * deviation * loudness
    return jnp.minimum(jnp.maximum(drawn, -bound), bound).astype(held_as)


def noise_with(own_key, extent, scale, limit, cuts, heavy, dtype=jnp.bfloat16):
    array = scale * jax.random.normal(own_key, extent, jnp.float32)
    if cuts:
        array = array * level_of(own_key, extent, cuts, -0.22, 0.18)
    return jnp.clip(strengthened(array, jax.random.fold_in(own_key, 3), *heavy), -limit, limit).astype(dtype)


def setup_inputs(seed: int = 0) -> dict:
    streams_of = jax.random.split(jax.random.key(seed), 8)
    tokens = noise(streams_of[0], (TOKENS, D), 1.0, 6.0, ((0, 256),))
    cotangent = noise(streams_of[1], (TOKENS, D), 1.0, 6.0, ((0, 256),))
    expert_ids_keys = jax.random.split(jax.random.fold_in(streams_of[2], 1), TOKENS // TOK_DEV)
    expert_ids_turns = jax.random.permutation(jax.random.fold_in(streams_of[2], 3), TOKENS // TOK_DEV)
    expert_ids = jax.vmap(lambda own, number: deal_out(jax.random.fold_in(streams_of[2], 2), own, number, TOK_DEV, EXPERTS, TOP, CAP, 1))(expert_ids_keys, expert_ids_turns).reshape((TOKENS, TOP))
    gate_probs = jnp.clip(0.2 + 0.8 * jax.random.uniform(streams_of[3], (TOKENS, TOP), jnp.float32) ** level_of(streams_of[3], (TOKENS, TOP), ((0, 256),), -0.2, 0.2), 0.2, 1.0)
    gate_up_weight = noise(streams_of[4], (EXPERTS, D, 2 * H_DEV), D ** -0.5, 0.125, ((0, 4),))
    down_weight = noise(streams_of[5], (EXPERTS, H_DEV, D), H_DEV ** -0.5, 0.25, ((0, 4),))
    down_residual = noise_with(streams_of[6], (DP_GROUPS, EXPERTS, H_DEV, D), 2.0, 32.0, ((0, 64), (1, 4)), (0, 2, 64, 4.0))
    return {"tokens": tokens, "cotangent": cotangent, "expert_ids": expert_ids, "gate_probs": gate_probs, "gate_up_weight": gate_up_weight, "down_weight": down_weight, "down_residual": down_residual}


def expert_forward(token_rows, gate_up):
    hidden_units = gate_up.shape[1] // 2
    projected = jnp.dot(token_rows, gate_up, preferred_element_type=jnp.float32)
    gate_part = projected[:, :hidden_units]
    up_part = projected[:, hidden_units:]
    gate_sig = jax.nn.sigmoid(gate_part)
    activated = gate_part * gate_sig
    hidden = (activated * up_part).astype(jnp.bfloat16)
    return gate_part, up_part, gate_sig, activated, hidden


def expert_backward(token_rows, scaled, forward, gate_up, down_matrix):
    gate_part, up_part, gate_sig, activated, hidden = forward
    back_hidden = jnp.dot(scaled, down_matrix.T, preferred_element_type=jnp.float32)
    back_gate = back_hidden * up_part * gate_sig * (1.0 + gate_part * (1.0 - gate_sig))
    back_up = back_hidden * activated
    back_both = jnp.concatenate([back_gate, back_up], axis=1).astype(jnp.bfloat16)
    token_part = jnp.dot(back_both, gate_up.T, preferred_element_type=jnp.float32).astype(jnp.bfloat16)
    contract = (((0,), (0,)), ((), ()))
    gate_up_term = lax.dot_general(token_rows, back_both, contract, preferred_element_type=jnp.float32)
    down_term = lax.dot_general(hidden, scaled, contract, preferred_element_type=jnp.float32)
    return token_part, gate_up_term, down_term


def round_trip(values):
    return lax.optimization_barrier(values.astype(jnp.bfloat16)).astype(jnp.float32)


def reference(tokens, cotangent, expert_ids, gate_probs, gate_up_weight, down_weight, down_residual):
    group_rows = TOKENS // DP_GROUPS

    def per_group(running, inputs):
        gate_up_sum, down_sum = running
        token_rows, grad_rows, routes, route_probs, residual = inputs
        token_sum = jnp.zeros((group_rows, D), jnp.float32)
        gate_up_list = []
        down_list = []
        for expert in range(EXPERTS):
            weight = jnp.sum(jnp.where(routes == expert, route_probs, jnp.zeros_like(route_probs)), axis=1)
            scaled = (grad_rows.astype(jnp.float32) * weight[:, None]).astype(jnp.bfloat16)
            forward = expert_forward(token_rows, gate_up_weight[expert])
            token_part, gate_up_term, down_term = expert_backward(token_rows, scaled, forward, gate_up_weight[expert], down_weight[expert])
            token_sum = token_sum + token_part.astype(jnp.float32)
            gate_up_list.append(round_trip(gate_up_term))
            down_list.append(round_trip(down_term + residual[expert].astype(jnp.float32)))
        gate_up_sum = gate_up_sum + jnp.stack(gate_up_list)
        down_sum = down_sum + jnp.stack(down_list)
        return (gate_up_sum, down_sum), token_sum.astype(jnp.bfloat16)

    start = (jnp.zeros((EXPERTS, D, 2 * H_DEV), jnp.float32), jnp.zeros((EXPERTS, H_DEV, D), jnp.float32))
    inputs = (tokens.reshape(DP_GROUPS, group_rows, D), cotangent.reshape(DP_GROUPS, group_rows, D), expert_ids.reshape(DP_GROUPS, group_rows, TOP), gate_probs.reshape(DP_GROUPS, group_rows, TOP), down_residual)
    (gate_up_sum, down_sum), token_parts = lax.scan(per_group, start, inputs)
    factor = 1.0 / DP_GROUPS
    return token_parts.reshape(TOKENS, D), gate_up_sum * factor, down_sum * factor
```

```python
import jax
import jax.numpy as jnp
from jax import lax
from jax.experimental import pallas as pl
from jax.experimental.pallas import tpu as pltpu
from jax.sharding import PartitionSpec as P

MESH = pl.DeviceIdType.MESH
CHIPS_Z, CHIPS_Y, CORES = 8, 4, 2
SHARE = 48
GATE_ROWS, DOWN_ROWS = 32, 8
WIDTH = 1024
COLS_A = 512
COLS_B = WIDTH - COLS_A
ORDER_Z = (4, 3, -3, 2, -2, 1, -1, 0)
ORDER_Y = (2, 1, -1, 0)


def scatter_kernel(
    gate_ref, down_ref, gate_out, down_out,
    give_a, give_b, got_a, got_b, own_a, own_b,
    az_buf, ay_buf, by_buf, bz_buf,
    pair_a_sem, pair_b_sem, az_sem, ay_sem, by_sem, bz_sem,
):
    me, col = lax.axis_index("dp"), lax.axis_index("expert")
    z, y, core = me // (CHIPS_Y * CORES), (me // CORES) % CHIPS_Y, me % CORES

    def at(zz, yy, cc):
        return (((zz + CHIPS_Z) % CHIPS_Z) * CHIPS_Y + (yy + CHIPS_Y) % CHIPS_Y) * CORES + cc

    def zi(off):
        return (z + off + CHIPS_Z) % CHIPS_Z

    def yi(off):
        return (y + off + CHIPS_Y) % CHIPS_Y

    partner = at(z, y, 1 - core)
    z_next, z_prev = at(z + 1, y, core), at(z - 1, y, core)
    y_next, y_prev = at(z, y + 1, core), at(z, y - 1, core)
    barrier = pltpu.get_barrier_semaphore()
    for device in (partner, z_next, z_prev, y_next, y_prev):
        pl.semaphore_signal(barrier, inc=1, device_id=(device, col), device_id_type=MESH)
    pl.semaphore_wait(barrier, 5)

    started = []

    def send(src, dst, sems, index, device):
        copy = pltpu.make_async_remote_copy(
            src_ref=src, dst_ref=dst, send_sem=sems.at[(0, *index)], recv_sem=sems.at[(1, *index)],
            device_id=(device, col), device_id_type=MESH,
        )
        copy.start()
        started.append(copy)
        return copy

    def term(zz, yy, cc, lo, hi):
        share = (zz * CHIPS_Y + yy) * CORES + cc
        gate_rows = pl.ds(pl.multiple_of(share * GATE_ROWS, GATE_ROWS), GATE_ROWS)
        down_rows = pl.ds(pl.multiple_of(share * DOWN_ROWS, DOWN_ROWS), DOWN_ROWS)
        low = jnp.concatenate(
            [down_ref[down_rows, lo:hi], down_ref[down_rows, WIDTH + lo : WIDTH + hi]], axis=0
        )
        return gate_ref[gate_rows, lo:hi], low

    def put(ref, index, values):
        gate_part, down_part = values
        ref[(*index, slice(0, 32))] = gate_part.astype(jnp.bfloat16)
        ref[(*index, slice(32, 48))] = down_part.astype(jnp.bfloat16)

    pair_copies = {}

    def give_group_a(off):
        def body(yy, carry):
            put(give_a, (zi(off), yy), term(zi(off), yy, 1 - core, 0, COLS_A))
            return carry
        lax.fori_loop(0, CHIPS_Y, body, 0)
        pair_copies["a", off] = send(
            give_a.at[zi(off)], got_a.at[zi(off)], pair_a_sem, (ORDER_Z.index(off),), partner
        )

    def give_group_b(off):
        def body(zz, carry):
            put(give_b, (yi(off), zz), term(zz, yi(off), 1 - core, COLS_A, WIDTH))
            return carry
        lax.fori_loop(0, CHIPS_Z, body, 0)
        pair_copies["b", off] = send(
            give_b.at[yi(off)], got_b.at[yi(off)], pair_b_sem, (ORDER_Y.index(off),), partner
        )

    def wide(value):
        return value.astype(jnp.float32)

    def take_group_a(off):
        pair_copies["a", off].wait_recv()
        def body(yy, carry):
            gate_part, down_part = term(zi(off), yy, core, 0, COLS_A)
            got = wide(got_a[zi(off), yy])
            put(own_a, (zi(off), yy), (gate_part + got[:32], down_part + got[32:]))
            return carry
        lax.fori_loop(0, CHIPS_Y, body, 0)

    def take_group_b(off):
        pair_copies["b", off].wait_recv()
        def body(zz, carry):
            gate_part, down_part = term(zz, yi(off), core, COLS_A, WIDTH)
            got = wide(got_b[yi(off), zz])
            put(own_b, (yi(off), zz), (gate_part + got[:32], down_part + got[32:]))
            return carry
        lax.fori_loop(0, CHIPS_Z, body, 0)

    def add_into(ref, index, part):
        ref[index] = (wide(ref[index]) + wide(part)).astype(jnp.bfloat16)

    copies = {}

    def a_z(side, step, yy, received):
        off = (5 - step) if side == 0 else step - 5
        if received:
            copies["az", side, step - 1, yy].wait_recv()
            add_into(own_a, (zi(off), yy), az_buf[side, step - 2, yy])
        copies["az", side, step, yy] = send(
            own_a.at[zi(off), yy], az_buf.at[side, step - 1, yy], az_sem, (side, step - 1, yy),
            z_next if side == 0 else z_prev,
        )

    def a_z_end(yy):
        total = wide(own_a[z, yy])
        for side in range(2):
            copies["az", side, 4, yy].wait_recv()
            total = total + wide(az_buf[side, 3, yy])
        own_a[z, yy] = total.astype(jnp.bfloat16)

    half_rows = {("ay", 0): slice(0, 32), ("ay", 1): slice(32, 48), ("bz", 0): slice(32, 48), ("bz", 1): slice(0, 32)}

    def a_y(side, step):
        off = (3 - step) if side == 0 else step - 3
        rows = half_rows["ay", side]
        if step == 1:
            copies["ay", side, 1] = send(
                own_a.at[z, yi(off), rows], ay_buf.at[side, 0, rows], ay_sem, (side, 0),
                y_next if side == 0 else y_prev,
            )
            return
        copies["ay", side, 1].wait_recv()
        add_into(own_a, (z, yi(off), rows), ay_buf[side, 0, rows])
        copies["ay", side, 2] = send(
            own_a.at[z, yi(off)], ay_buf.at[side, 1], ay_sem, (side, 1),
            y_next if side == 0 else y_prev,
        )

    def finish(total, lo):
        total = total * (1.0 / (CHIPS_Z * CHIPS_Y * CORES))
        width = total.shape[1]
        gate_out[:, lo : lo + width] = total[:32]
        down_out[:, lo : lo + width] = total[32:40]
        down_out[:, WIDTH + lo : WIDTH + lo + width] = total[40:48]

    def a_end():
        total = wide(own_a[z, y])
        for side in range(2):
            copies["ay", side, 2].wait_recv()
            total = total + wide(ay_buf[side, 1])
        finish(total, 0)

    def b_y(side, step, piece, received):
        off = (3 - step) if side == 0 else step - 3
        at_z = zi(piece)
        slot = ORDER_Z.index(piece)
        if received:
            copies["by", side, step - 1, piece].wait_recv()
            add_into(own_b, (yi(off), at_z), by_buf[side, step - 2, slot])
        copies["by", side, step, piece] = send(
            own_b.at[yi(off), at_z], by_buf.at[side, step - 1, slot], by_sem, (side, step - 1, slot),
            y_next if side == 0 else y_prev,
        )

    def b_y_end(piece):
        total = wide(own_b[y, zi(piece)])
        for side in range(2):
            copies["by", side, 2, piece].wait_recv()
            total = total + wide(by_buf[side, 1, ORDER_Z.index(piece)])
        own_b[y, zi(piece)] = total.astype(jnp.bfloat16)

    def b_z(side, step):
        off = (5 - step) if side == 0 else step - 5
        rows = half_rows["bz", side] if step == 1 else slice(0, 48)
        if step > 1:
            before = half_rows["bz", side] if step == 2 else slice(0, 48)
            copies["bz", side, step - 1].wait_recv()
            add_into(own_b, (y, zi(off), before), bz_buf[side, step - 2, before])
        copies["bz", side, step] = send(
            own_b.at[y, zi(off), rows], bz_buf.at[side, step - 1, rows], bz_sem, (side, step - 1),
            z_next if side == 0 else z_prev,
        )

    def b_end():
        total = wide(own_b[y, z])
        for side in range(2):
            copies["bz", side, 4].wait_recv()
            total = total + wide(bz_buf[side, 3])
        finish(total, COLS_A)

    upper, lower = (4, 3, 2, 1), (-3, -2, -1, 0)
    first = {0: (0, 1), 1: (2, 3)}
    early_b = {0: upper, 1: lower}

    give_group_a(4)
    give_group_a(3)
    give_group_a(-3)
    give_group_b(2)
    give_group_b(1)
    give_group_b(-1)
    take_group_a(4)
    for piece in range(2):
        for side in range(2):
            a_z(side, 1, first[side][piece], False)
    give_group_a(2)
    give_group_a(-2)
    take_group_a(3)
    take_group_a(-3)
    for piece in range(2):
        for side in range(2):
            a_z(side, 2, first[1 - side][piece], False)
    take_group_b(2)
    for piece in range(4):
        for side in range(2):
            b_y(side, 1, early_b[side][piece], False)
    give_group_b(0)
    give_group_a(1)
    give_group_a(-1)
    give_group_a(0)
    take_group_b(1)
    take_group_b(-1)
    for piece in range(4):
        for side in range(2):
            b_y(side, 2, early_b[1 - side][piece], False)
    for piece in range(2):
        for side in range(2):
            a_z(side, 2, first[side][piece], True)
    take_group_a(2)
    take_group_a(-2)
    for piece in range(2):
        for side in range(2):
            a_z(side, 3, first[1 - side][piece], True)
    for piece in range(2):
        for side in range(2):
            b_y(side, 2, early_b[side][piece], True)
    take_group_a(1)
    take_group_a(-1)
    for piece in range(2):
        for side in range(2):
            a_z(side, 3, first[side][piece], True)
    for piece in range(2, 4):
        for side in range(2):
            b_y(side, 2, early_b[side][piece], True)
    take_group_b(0)
    take_group_a(0)
    for piece in range(2):
        for side in range(2):
            a_z(side, 4, first[1 - side][piece], True)
    b_y_end(4)
    for side in range(2):
        b_z(side, 1)
    for piece in range(2):
        for side in range(2):
            a_z(side, 4, first[side][piece], True)
    b_y_end(3)
    b_y_end(-3)
    for side in range(2):
        b_z(side, 2)
    b_y_end(2)
    b_y_end(-2)
    for side in range(2):
        b_z(side, 3)
    b_y_end(1)
    b_y_end(-1)
    b_y_end(0)
    for yy in (2, 3, 0, 1):
        a_z_end(yy)
    for side in range(2):
        a_y(side, 1)
    for side in range(2):
        b_z(side, 4)
    for side in range(2):
        a_y(side, 2)
    b_end()
    a_end()
    for copy in started:
        copy.wait_send()


def reduce_scatter(gate_up_term, down_term):
    bf16 = jnp.bfloat16
    sems = pltpu.SemaphoreType.DMA
    vmem = pl.BlockSpec(memory_space=pltpu.VMEM)
    return pl.pallas_call(
        scatter_kernel,
        out_shape=(
            jax.ShapeDtypeStruct((GATE_ROWS, WIDTH), jnp.float32),
            jax.ShapeDtypeStruct((DOWN_ROWS, 2 * WIDTH), jnp.float32),
        ),
        in_specs=[vmem, vmem],
        out_specs=(vmem, vmem),
        scratch_shapes=[
            pltpu.VMEM((CHIPS_Z, CHIPS_Y, SHARE, COLS_A), bf16),
            pltpu.VMEM((CHIPS_Y, CHIPS_Z, SHARE, COLS_B), bf16),
            pltpu.VMEM((CHIPS_Z, CHIPS_Y, SHARE, COLS_A), bf16),
            pltpu.VMEM((CHIPS_Y, CHIPS_Z, SHARE, COLS_B), bf16),
            pltpu.VMEM((CHIPS_Z, CHIPS_Y, SHARE, COLS_A), bf16),
            pltpu.VMEM((CHIPS_Y, CHIPS_Z, SHARE, COLS_B), bf16),
            pltpu.VMEM((2, 4, CHIPS_Y, SHARE, COLS_A), bf16),
            pltpu.VMEM((2, 2, SHARE, COLS_A), bf16),
            pltpu.VMEM((2, 2, CHIPS_Z, SHARE, COLS_B), bf16),
            pltpu.VMEM((2, 4, SHARE, COLS_B), bf16),
            sems((2, 8)),
            sems((2, 4)),
            sems((2, 2, 4, 4)),
            sems((2, 2, 2)),
            sems((2, 2, 2, 8)),
            sems((2, 2, 4)),
        ],
        compiler_params=pltpu.CompilerParams(
            collective_id=0, has_side_effects=True, vmem_limit_bytes=60 * 1024 * 1024
        ),
    )(gate_up_term, down_term)


def expert_forward(token_rows, gate_up):
    hidden_units = gate_up.shape[1] // 2
    projected = jnp.dot(token_rows, gate_up, preferred_element_type=jnp.float32)
    gate_part = projected[:, :hidden_units]
    up_part = projected[:, hidden_units:]
    gate_sig = jax.nn.sigmoid(gate_part)
    activated = gate_part * gate_sig
    hidden = (activated * up_part).astype(jnp.bfloat16)
    return (gate_part, up_part, gate_sig, activated, hidden)


def expert_backward(token_rows, scaled, forward, gate_up, down_matrix):
    gate_part, up_part, gate_sig, activated, hidden = forward
    back_hidden = jnp.dot(scaled, down_matrix.T, preferred_element_type=jnp.float32)
    back_gate = back_hidden * up_part * gate_sig * (1.0 + gate_part * (1.0 - gate_sig))
    back_up = back_hidden * activated
    back_both = jnp.concatenate([back_gate, back_up], axis=1).astype(jnp.bfloat16)
    token_part = jnp.dot(back_both, gate_up.T, preferred_element_type=jnp.float32).astype(
        jnp.bfloat16
    )
    contract = (((0,), (0,)), ((), ()))
    gate_up_term = lax.dot_general(
        token_rows, back_both, contract, preferred_element_type=jnp.float32
    )
    down_term = lax.dot_general(hidden, scaled, contract, preferred_element_type=jnp.float32)
    return (token_part, gate_up_term, down_term)


def on_device(
    tokens, cotangent, expert_ids, gate_probs, gate_up_weight, down_weight, down_residual
):
    tok_rows, model_width = tokens.shape
    expert_count = lax.axis_size("expert")
    capacity = tok_rows * 5 // 8
    expert_range = jnp.arange(expert_count, dtype=jnp.int32)
    route_hit = expert_ids[:, :, None] == expert_range[None, None, :]
    member = jnp.any(route_hit, axis=1).astype(jnp.int32)
    route_weight = jnp.sum(jnp.where(route_hit, gate_probs[:, :, None], 0.0), axis=1)
    slot_index = jnp.cumsum(member, axis=0) - member
    slot_range = jnp.arange(capacity, dtype=jnp.int32)
    placed = (member.T[:, None, :] == 1) & (slot_index.T[:, None, :] == slot_range[None, :, None])
    token_range = jnp.arange(tok_rows, dtype=jnp.int32)
    filled = jnp.any(placed, axis=2)
    source_row = jnp.where(
        filled, jnp.sum(jnp.where(placed, token_range[None, None, :], 0), axis=2), tok_rows
    )
    slot_weight = jnp.sum(jnp.where(placed, route_weight.T[:, None, :], 0.0), axis=2)
    zero_row = jnp.zeros((1, model_width), jnp.bfloat16)
    send_rows = jnp.concatenate([tokens, zero_row], axis=0)[source_row]
    send_grads = (
        jnp.concatenate([cotangent, zero_row], axis=0)[source_row].astype(jnp.float32)
        * slot_weight[:, :, None]
    ).astype(jnp.bfloat16)
    gate_up = gate_up_weight[0]
    down_matrix = down_weight[0]
    total_rows = expert_count * capacity
    got_rows, got_grads = (
        lax.all_to_all(send_rows, "expert", split_axis=0, concat_axis=0, tiled=True),
        lax.all_to_all(send_grads, "expert", split_axis=0, concat_axis=0, tiled=True),
    )
    flat_rows = got_rows.reshape(total_rows, model_width)
    forward = expert_forward(flat_rows, gate_up)
    flat_grads = got_grads.reshape(total_rows, model_width)
    token_part, gate_up_term, down_term = expert_backward(
        flat_rows, flat_grads, forward, gate_up, down_matrix
    )
    returned = lax.all_to_all(
        token_part.reshape(expert_count, capacity, model_width),
        "expert",
        split_axis=0,
        concat_axis=0,
        tiled=True,
    )
    returned = returned.reshape(total_rows, model_width)
    pick_rows = expert_ids * capacity + jnp.take_along_axis(slot_index, expert_ids, axis=1)
    token_grad = jnp.sum(returned[pick_rows].astype(jnp.float32), axis=1).astype(jnp.bfloat16)
    gate_up_part, down_part = reduce_scatter(
        gate_up_term, down_term + down_residual[0, 0].astype(jnp.float32)
    )
    return (token_grad, gate_up_part[None], down_part[None])


def solution(mesh):
    placed = (
        P(("dp", "expert"), None),
        P(("dp", "expert"), None),
        P(("dp", "expert"), None),
        P(("dp", "expert"), None),
        P("expert", None, None),
        P("expert", None, None),
        P("dp", "expert", None, None),
    )
    return jax.shard_map(
        on_device,
        mesh=mesh,
        in_specs=placed,
        out_specs=(P(("dp", "expert"), None), P("expert", "dp", None), P("expert", "dp", None)),
        check_vma=False,
    )
```

```python
import jax
import jax.numpy as jnp
from jax import lax
from jax.experimental import pallas as pl
from jax.experimental.pallas import tpu as pltpu
from jax.sharding import PartitionSpec as P

MESH = pl.DeviceIdType.MESH
CHIPS_Z, CHIPS_Y, CORES, EXPERTS = 8, 4, 2, 4
SHARE = 48
GATE_ROWS, DOWN_ROWS = 32, 8
WIDTH = 1024
COLS_A = 512
COLS_B = WIDTH - COLS_A
ORDER_Z = (4, 3, -3, 2, -2, 1, -1, 0)
ORDER_Y = (2, 1, -1, 0)
TOK, CAP, MODEL, UNITS = 128, 80, 2048, 512
ROWS = EXPERTS * CAP
OPP, SELF, LOW, HIGH = (slice(k * CAP, (k + 1) * CAP) for k in range(4))
EARLY, LATE, NEAR = slice(0, 2 * CAP), slice(2 * CAP, ROWS), slice(CAP, ROWS)


def wide(value):
    return value.astype(jnp.float32)


def dot(left, right):
    return jnp.dot(left, right, preferred_element_type=jnp.float32)


def dot_rows(left, right):
    return lax.dot_general(left, right, (((0,), (0,)), ((), ())), preferred_element_type=jnp.float32)


def columns(index, width):
    return pl.ds(pl.multiple_of(index * width, width), width)


def loop(count, body):
    def step(index, carry):
        body(index)
        return carry

    lax.fori_loop(0, count, step, 0)


def layer_kernel(
    ids_ref, probs_ref, tokens_hbm, cotangent_hbm, gate_up_hbm, down_hbm, residual_hbm,
    token_out, gate_out, down_out,
    tok_in, cot_in, gate_up, down, residual, gate_up_t, down_t,
    place, slot_weight, tok_send, grad_send, tok_relay, grad_relay,
    tok_all, grad_all, both, back, hidden, sum_gate, sum_down,
    part, part_relay, returned,
    half_a, half_b, got_a, got_b, az_buf, ay_buf, by_buf, bz_buf,
    load_sem, swap_sem, return_sem,
    pair_a_sem, pair_b_sem, az_sem, ay_sem, by_sem, bz_sem,
):
    bf16 = jnp.bfloat16
    me, x = lax.axis_index("dp"), lax.axis_index("expert")
    z, y, core = me // (CHIPS_Y * CORES), (me // CORES) % CHIPS_Y, me % CORES

    def at(zz, yy, cc):
        return (((zz + CHIPS_Z) % CHIPS_Z) * CHIPS_Y + (yy + CHIPS_Y) % CHIPS_Y) * CORES + cc

    def zi(off):
        return (z + off + CHIPS_Z) % CHIPS_Z

    def yi(off):
        return (y + off + CHIPS_Y) % CHIPS_Y

    partner = (at(z, y, 1 - core), x)
    z_side = ((at(z + 1, y, core), x), (at(z - 1, y, core), x))
    y_side = ((at(z, y + 1, core), x), (at(z, y - 1, core), x))
    x_side = ((me, (x + 1) % EXPERTS), (me, (x + EXPERTS - 1) % EXPERTS))
    barrier = pltpu.get_barrier_semaphore()
    for device in (partner, *z_side, *y_side, *x_side):
        pl.semaphore_signal(barrier, inc=1, device_id=device, device_id_type=MESH)

    loads = [
        pltpu.make_async_copy(source, target, load_sem.at[k])
        for k, (source, target) in enumerate(
            (
                (tokens_hbm, tok_in),
                (cotangent_hbm, cot_in),
                (down_hbm, down),
                (gate_up_hbm, gate_up),
                (residual_hbm, residual),
            )
        )
    ]
    for copy in loads:
        copy.start()

    started = []

    def send(src, dst, sems, index, device):
        copy = pltpu.make_async_remote_copy(
            src_ref=src, dst_ref=dst, send_sem=sems.at[(0, *index)], recv_sem=sems.at[(1, *index)],
            device_id=device, device_id_type=MESH,
        )
        copy.start()
        started.append(copy)
        return copy

    ids, probs = ids_ref[...], probs_ref[...]
    before = lax.broadcasted_iota(jnp.int32, (TOK, TOK), 0) < lax.broadcasted_iota(jnp.int32, (TOK, TOK), 1)
    before = jnp.where(before, 1.0, 0.0).astype(bf16)
    slots = wide(lax.broadcasted_iota(jnp.int32, (CAP, TOK), 0))
    for k in range(EXPERTS):
        expert = (x + k) % EXPERTS
        hits = ids == expert
        member = jnp.sum(jnp.where(hits, 1.0, 0.0), axis=0, keepdims=True)
        weight = jnp.sum(jnp.where(hits, probs, 0.0), axis=0, keepdims=True)
        index = dot(jnp.broadcast_to(member, (8, TOK)).astype(bf16), before)[0:1]
        chosen = jnp.where((slots == index) & (member > 0.5), 1.0, 0.0)
        rows = slice(k * CAP, (k + 1) * CAP)
        place[rows] = chosen.astype(bf16)
        slot_weight[rows] = jnp.broadcast_to(jnp.sum(chosen * weight, axis=1, keepdims=True), (CAP, TOK))

    def pick_tokens(k, target, rows):
        def body(n):
            cols = columns(n, 512)
            target[rows, cols] = dot(place[k * CAP : (k + 1) * CAP], tok_in[:, cols]).astype(bf16)
        loop(4, body)

    def pick_grads(k, target, rows):
        def body(n):
            cols = columns(n, 512)
            block = slice(k * CAP, (k + 1) * CAP)
            value = dot(place[block], cot_in[:, cols]) * slot_weight[block, 0:1]
            target[rows, cols] = value.astype(bf16)
        loop(4, body)

    swap = {}
    first, second, third = slice(0, CAP), slice(CAP, 2 * CAP), slice(2 * CAP, 3 * CAP)
    loads[0].wait()
    pick_tokens(2, tok_send, second)
    pl.semaphore_wait(barrier, 7)
    swap["tok", "leg"] = send(tok_send.at[second], tok_relay, swap_sem, (0,), x_side[0])
    loads[1].wait()
    pick_grads(2, grad_send, second)
    swap["grad", "leg"] = send(grad_send.at[second], grad_relay, swap_sem, (1,), x_side[1])
    pick_tokens(1, tok_send, first)
    swap["tok", 0] = send(tok_send.at[first], tok_all.at[LOW], swap_sem, (2,), x_side[0])
    pick_tokens(3, tok_send, third)
    swap["tok", 1] = send(tok_send.at[third], tok_all.at[HIGH], swap_sem, (3,), x_side[1])
    pick_grads(1, grad_send, first)
    pick_grads(3, grad_send, third)
    pick_tokens(0, tok_all, SELF)
    pick_grads(0, grad_all, SELF)
    loads[2].wait()

    def turn_down(n):
        rows = columns(n, 256)
        down_t[rows, :] = down[:, rows].T

    loop(8, turn_down)
    swap["tok", "leg"].wait_recv()
    swap["tok", "far"] = send(tok_relay, tok_all.at[OPP], swap_sem, (4,), x_side[0])
    swap["grad", "leg"].wait_recv()
    swap["grad", "far"] = send(grad_relay, grad_all.at[OPP], swap_sem, (5,), x_side[1])
    swap["grad", 0] = send(grad_send.at[first], grad_all.at[LOW], swap_sem, (6,), x_side[0])
    swap["grad", 1] = send(grad_send.at[third], grad_all.at[HIGH], swap_sem, (7,), x_side[1])
    loads[3].wait()

    def turn_gate_up(n):
        rows = columns(n, 256)
        gate_up_t[:, rows] = gate_up[rows, :].T

    loop(8, turn_gate_up)
    loads[4].wait()

    def project(rows):
        def body(n):
            cols = columns(n, 256)
            both[rows, cols] = dot(tok_all[rows], gate_up[:, cols])
        loop(4, body)

        def gates(n):
            r = pl.ds(pl.multiple_of(rows.start + n * 16, 16), 16)
            gate, up = both[r, 0:UNITS], both[r, UNITS : 2 * UNITS]
            sig = jax.nn.sigmoid(gate)
            active = gate * sig
            hidden[r] = (active * up).astype(bf16)
            both[r, 0:UNITS] = up * sig * (1.0 + gate * (1.0 - sig))
            both[r, UNITS : 2 * UNITS] = active
        loop((rows.stop - rows.start) // 16, gates)

    def pull_back(rows):
        def body(n):
            cols, upper = columns(n, 256), columns(n + 2, 256)
            value = dot(grad_all[rows], down_t[:, cols])
            back[rows, cols] = (value * both[rows, cols]).astype(bf16)
            back[rows, upper] = (value * both[rows, upper]).astype(bf16)
        loop(2, body)

    swap["tok", 0].wait_recv()
    swap["tok", 1].wait_recv()
    project(NEAR)
    swap["tok", "far"].wait_recv()
    project(OPP)
    swap["grad", "far"].wait_recv()
    pull_back(EARLY)

    def early_gate(n):
        rows = columns(n, 256)
        turned = tok_all[EARLY, rows].T
        for half in range(2):
            cols = slice(half * 512, half * 512 + 512)
            sum_gate[rows, cols] = dot(turned, back[EARLY, cols])
    loop(8, early_gate)

    def early_down(n):
        rows = columns(n, 128)
        turned = hidden[EARLY, rows].T
        for half in range(4):
            cols = slice(half * 512, half * 512 + 512)
            sum_down[rows, cols] = dot(turned, grad_all[EARLY, cols]) + wide(residual[rows, cols])
    loop(4, early_down)

    swap["grad", 0].wait_recv()
    swap["grad", 1].wait_recv()
    pull_back(LATE)

    def late_down(n):
        rows = columns(n, 128)
        turned = hidden[LATE, rows].T
        for half in range(4):
            cols = slice(half * 512, half * 512 + 512)
            sum_down[rows, cols] += dot(turned, grad_all[LATE, cols])
    loop(4, late_down)

    def pair_a(k, zz):
        return pltpu.make_async_remote_copy(
            src_ref=half_a.at[1 - core, zz], dst_ref=got_a.at[zz],
            send_sem=pair_a_sem.at[0, k], recv_sem=pair_a_sem.at[1, k],
            device_id=partner, device_id_type=MESH,
        )

    def late_gate(k):
        zz = (z + 4 + ((k + 1) // 2) * (1 - 2 * ((k + 1) % 2)) + CHIPS_Z) % CHIPS_Z
        rows = columns(zz, 256)
        turned = tok_all[LATE, rows].T
        down_rows = [
            pl.ds(pl.multiple_of(zz * 64 + part_at * 8, 8), 8) for part_at in range(8)
        ]
        for half, lo in ((half_a, 0), (half_b, COLS_A)):
            hi = lo + (COLS_A if half is half_a else COLS_B)
            value = sum_gate[rows, lo:hi] + dot(turned, back[LATE, lo:hi])
            for yy in range(CHIPS_Y):
                for cc in range(CORES):
                    index = yy * CORES + cc
                    slot = (cc, zz, yy) if half is half_a else (cc, yy, zz)
                    half[(*slot, slice(0, 32))] = value[32 * index : 32 * index + 32].astype(bf16)
                    low = jnp.concatenate(
                        [
                            sum_down[down_rows[index], lo:hi],
                            sum_down[down_rows[index], WIDTH + lo : WIDTH + hi],
                        ],
                        axis=0,
                    )
                    half[(*slot, slice(32, 48))] = low.astype(bf16)
        pair_a(k, zz).start()

    loop(8, late_gate)
    pair_copies = {("a", off): pair_a(ORDER_PAIR.index(off), zi(off)) for off in ORDER_Z}
    started.extend(pair_copies.values())
    for off in ORDER_Y:
        pair_copies["b", off] = send(
            half_b.at[1 - core, yi(off)], got_b.at[yi(off)], pair_b_sem, (ORDER_Y.index(off),), partner
        )
    own_a, own_b = half_a.at[core], half_b.at[core]

    def take_group_a(off):
        pair_copies["a", off].wait_recv()

        def body(yy):
            own_a[zi(off), yy] = (wide(own_a[zi(off), yy]) + wide(got_a[zi(off), yy])).astype(bf16)
        loop(CHIPS_Y, body)

    def take_group_b(off):
        pair_copies["b", off].wait_recv()

        def body(zz):
            own_b[yi(off), zz] = (wide(own_b[yi(off), zz]) + wide(got_b[yi(off), zz])).astype(bf16)
        loop(CHIPS_Z, body)

    back_copies = {}

    def token_columns(n):
        cols = slice(n * 256, n * 256 + 256)
        value = dot(back[...], gate_up_t[:, cols]).astype(bf16)
        part[:, cols] = value
        returned[0:CAP, cols] = value[SELF]

    def give_back(half):
        cols = slice(half * 1024, half * 1024 + 1024)
        other = x_side[half]
        back_copies["high", half] = send(
            part.at[HIGH, cols], returned.at[3 * CAP : 4 * CAP, cols], return_sem, (half, 0), x_side[0]
        )
        back_copies["low", half] = send(
            part.at[LOW, cols], returned.at[CAP : 2 * CAP, cols], return_sem, (half, 1), x_side[1]
        )
        back_copies["leg", half] = send(
            part.at[OPP, cols], part_relay.at[half], return_sem, (half, 2), other
        )

    def pass_on(half):
        cols = slice(half * 1024, half * 1024 + 1024)
        back_copies["leg", half].wait_recv()
        back_copies["far", half] = send(
            part_relay.at[half], returned.at[2 * CAP : 3 * CAP, cols], return_sem, (half, 3), x_side[half]
        )

    def combine():
        for half in range(2):
            for name in ("high", "low", "far"):
                back_copies[name, half].wait_recv()

        def body(n):
            cols = columns(n, 256)
            token_out[:, cols] = dot_rows(place[...], returned[:, cols]).astype(bf16)
        loop(8, body)

    def add_into(ref, index, part):
        ref[index] = (wide(ref[index]) + wide(part)).astype(jnp.bfloat16)

    copies = {}

    def a_z(side, step, yy, received):
        off = (5 - step) if side == 0 else step - 5
        if received:
            copies["az", side, step - 1, yy].wait_recv()
            add_into(own_a, (zi(off), yy), az_buf[side, step - 2, yy])
        copies["az", side, step, yy] = send(
            own_a.at[zi(off), yy], az_buf.at[side, step - 1, yy], az_sem, (side, step - 1, yy),
            z_side[side],
        )

    def a_z_end(yy):
        total = wide(own_a[z, yy])
        for side in range(2):
            copies["az", side, 4, yy].wait_recv()
            total = total + wide(az_buf[side, 3, yy])
        own_a[z, yy] = total.astype(jnp.bfloat16)

    half_rows = {("ay", 0): slice(0, 32), ("ay", 1): slice(32, 48), ("bz", 0): slice(32, 48), ("bz", 1): slice(0, 32)}

    def a_y(side, step):
        off = (3 - step) if side == 0 else step - 3
        rows = half_rows["ay", side]
        if step == 1:
            copies["ay", side, 1] = send(
                own_a.at[z, yi(off), rows], ay_buf.at[side, 0, rows], ay_sem, (side, 0),
                y_side[side],
            )
            return
        copies["ay", side, 1].wait_recv()
        add_into(own_a, (z, yi(off), rows), ay_buf[side, 0, rows])
        copies["ay", side, 2] = send(
            own_a.at[z, yi(off)], ay_buf.at[side, 1], ay_sem, (side, 1),
            y_side[side],
        )

    def finish(total, lo):
        total = total * (1.0 / (CHIPS_Z * CHIPS_Y * CORES))
        width = total.shape[1]
        gate_out[:, lo : lo + width] = total[:32]
        down_out[:, lo : lo + width] = total[32:40]
        down_out[:, WIDTH + lo : WIDTH + lo + width] = total[40:48]

    def a_end():
        total = wide(own_a[z, y])
        for side in range(2):
            copies["ay", side, 2].wait_recv()
            total = total + wide(ay_buf[side, 1])
        finish(total, 0)

    def b_y(side, step, piece, received):
        off = (3 - step) if side == 0 else step - 3
        at_z = zi(piece)
        slot = ORDER_Z.index(piece)
        if received:
            copies["by", side, step - 1, piece].wait_recv()
            add_into(own_b, (yi(off), at_z), by_buf[side, step - 2, slot])
        copies["by", side, step, piece] = send(
            own_b.at[yi(off), at_z], by_buf.at[side, step - 1, slot], by_sem, (side, step - 1, slot),
            y_side[side],
        )

    def b_y_end(piece):
        total = wide(own_b[y, zi(piece)])
        for side in range(2):
            copies["by", side, 2, piece].wait_recv()
            total = total + wide(by_buf[side, 1, ORDER_Z.index(piece)])
        own_b[y, zi(piece)] = total.astype(jnp.bfloat16)

    def b_z(side, step):
        off = (5 - step) if side == 0 else step - 5
        rows = half_rows["bz", side] if step == 1 else slice(0, 48)
        if step > 1:
            before = half_rows["bz", side] if step == 2 else slice(0, 48)
            copies["bz", side, step - 1].wait_recv()
            add_into(own_b, (y, zi(off), before), bz_buf[side, step - 2, before])
        copies["bz", side, step] = send(
            own_b.at[y, zi(off), rows], bz_buf.at[side, step - 1, rows], bz_sem, (side, step - 1),
            z_side[side],
        )

    def b_end():
        total = wide(own_b[y, z])
        for side in range(2):
            copies["bz", side, 4].wait_recv()
            total = total + wide(bz_buf[side, 3])
        finish(total, COLS_A)

    upper, lower = (4, 3, 2, 1), (-3, -2, -1, 0)
    edge = {0: (0, 1), 1: (2, 3)}
    early_b = {0: upper, 1: lower}

    def pieces_a(step, fresh, received):
        for piece in range(2):
            for side in range(2):
                a_z(side, step, edge[1 - side if fresh else side][piece], received)

    def pieces_b(step, fresh, received, which):
        for piece in which:
            for side in range(2):
                b_y(side, step, early_b[1 - side if fresh else side][piece], received)

    def both_sides(action, step):
        for side in range(2):
            action(side, step)

    take_group_a(4)
    pieces_a(1, False, False)
    take_group_a(3)
    take_group_a(-3)
    pieces_a(2, True, False)
    take_group_b(2)
    pieces_b(1, False, False, range(4))
    take_group_b(1)
    take_group_b(-1)
    pieces_b(2, True, False, range(4))
    token_columns(0)
    token_columns(1)
    pieces_a(2, False, True)
    token_columns(2)
    token_columns(3)
    give_back(0)
    take_group_a(2)
    take_group_a(-2)
    pieces_a(3, True, True)
    pieces_b(2, False, True, range(2))
    token_columns(4)
    token_columns(5)
    take_group_a(1)
    take_group_a(-1)
    pieces_a(3, False, True)
    pieces_b(2, False, True, range(2, 4))
    token_columns(6)
    token_columns(7)
    give_back(1)
    take_group_b(0)
    take_group_a(0)
    pieces_a(4, True, True)
    b_y_end(4)
    both_sides(b_z, 1)
    pieces_a(4, False, True)
    pass_on(0)
    b_y_end(3)
    b_y_end(-3)
    both_sides(b_z, 2)
    b_y_end(2)
    b_y_end(-2)
    both_sides(b_z, 3)
    b_y_end(1)
    b_y_end(-1)
    b_y_end(0)
    pass_on(1)
    for yy in (2, 3, 0, 1):
        a_z_end(yy)
    both_sides(a_y, 1)
    both_sides(b_z, 4)
    both_sides(a_y, 2)
    combine()
    b_end()
    a_end()
    for copy in started:
        copy.wait_send()


ORDER_PAIR = (4, -3, 3, -2, 2, -1, 1, 0)


def on_device(
    tokens, cotangent, expert_ids, gate_probs, gate_up_weight, down_weight, down_residual
):
    bf16, f32 = jnp.bfloat16, jnp.float32
    sems = pltpu.SemaphoreType.DMA
    vmem, anywhere = pl.BlockSpec(memory_space=pltpu.VMEM), pl.BlockSpec(memory_space=pl.ANY)
    shapes = (
        ((TOK, MODEL), bf16), ((TOK, MODEL), bf16), ((MODEL, WIDTH), bf16), ((UNITS, MODEL), bf16),
        ((UNITS, MODEL), bf16), ((WIDTH, MODEL), bf16), ((MODEL, UNITS), bf16),
        ((ROWS, TOK), bf16), ((ROWS, TOK), f32), ((3 * CAP, MODEL), bf16), ((3 * CAP, MODEL), bf16),
        ((CAP, MODEL), bf16), ((CAP, MODEL), bf16),
        ((ROWS, MODEL), bf16), ((ROWS, MODEL), bf16), ((ROWS, WIDTH), f32), ((ROWS, WIDTH), bf16),
        ((ROWS, UNITS), bf16), ((MODEL, WIDTH), f32), ((UNITS, MODEL), f32),
        ((ROWS, MODEL), bf16), ((2, CAP, MODEL // 2), bf16), ((ROWS, MODEL), bf16),
        ((CORES, CHIPS_Z, CHIPS_Y, SHARE, COLS_A), bf16), ((CORES, CHIPS_Y, CHIPS_Z, SHARE, COLS_B), bf16),
        ((CHIPS_Z, CHIPS_Y, SHARE, COLS_A), bf16), ((CHIPS_Y, CHIPS_Z, SHARE, COLS_B), bf16),
        ((2, 4, CHIPS_Y, SHARE, COLS_A), bf16), ((2, 2, SHARE, COLS_A), bf16),
        ((2, 2, CHIPS_Z, SHARE, COLS_B), bf16), ((2, 4, SHARE, COLS_B), bf16),
    )
    semaphores = ((5,), (2, 8), (2, 2, 4), (2, 8), (2, 4), (2, 2, 4, 4), (2, 2, 2), (2, 2, 2, 8), (2, 2, 4))
    token_grad, gate_up_part, down_part = pl.pallas_call(
        layer_kernel,
        out_shape=(
            jax.ShapeDtypeStruct((TOK, MODEL), bf16),
            jax.ShapeDtypeStruct((GATE_ROWS, WIDTH), f32),
            jax.ShapeDtypeStruct((DOWN_ROWS, MODEL), f32),
        ),
        in_specs=[vmem, vmem, anywhere, anywhere, anywhere, anywhere, anywhere],
        out_specs=(vmem, vmem, vmem),
        scratch_shapes=[pltpu.VMEM(*shape) for shape in shapes] + [sems(shape) for shape in semaphores],
        compiler_params=pltpu.CompilerParams(
            collective_id=0, has_side_effects=True, vmem_limit_bytes=62 * 1024 * 1024
        ),
    )(
        expert_ids.T, gate_probs.T, tokens, cotangent, gate_up_weight[0], down_weight[0], down_residual[0, 0]
    )
    return (token_grad, gate_up_part[None], down_part[None])


def solution(mesh):
    placed = (
        P(("dp", "expert"), None),
        P(("dp", "expert"), None),
        P(("dp", "expert"), None),
        P(("dp", "expert"), None),
        P("expert", None, None),
        P("expert", None, None),
        P("dp", "expert", None, None),
    )
    return jax.shard_map(
        on_device,
        mesh=mesh,
        in_specs=placed,
        out_specs=(P(("dp", "expert"), None), P("expert", "dp", None), P("expert", "dp", None)),
        check_vma=False,
    )
```

```python
import jax
import jax.numpy as jnp
from jax import lax
from jax.experimental import pallas as pl
from jax.experimental.pallas import tpu as pltpu
from jax.sharding import PartitionSpec as P

MESH = pl.DeviceIdType.MESH
CHIPS_Z, CHIPS_Y, CORES, EXPERTS = 8, 4, 2, 4
SHARE, WIDTH, HALF = 96, 1024, 512
GATE_ROWS, DOWN_ROWS = 32, 8
ROWS_A = 48
ROWS_B = SHARE - ROWS_A
FAR_PARTS = ((0, 32), (32, ROWS_B))
GROUPS = (4, -3, 3, -2, 2, -1, 1, 0)
ORDER_Y = (2, 1, -1, 0)
TOK, CAP, MODEL, UNITS = 128, 80, 2048, 512
ROWS = EXPERTS * CAP
OPP, SELF, LOW, HIGH = (slice(k * CAP, (k + 1) * CAP) for k in range(4))
EARLY, LATE, NEAR = slice(0, 2 * CAP), slice(2 * CAP, ROWS), slice(CAP, ROWS)


def wide(value):
    return value.astype(jnp.float32)


def dot(left, right):
    return jnp.dot(left, right, preferred_element_type=jnp.float32)


def dot_rows(left, right):
    return lax.dot_general(left, right, (((0,), (0,)), ((), ())), preferred_element_type=jnp.float32)


def columns(index, width):
    return pl.ds(pl.multiple_of(index * width, width), width)


def loop(count, body):
    def step(index, carry):
        body(index)
        return carry

    lax.fori_loop(0, count, step, 0)


def layer_kernel(
    ids_hbm, probs_hbm, tokens_hbm, cotangent_hbm, gate_up_hbm, down_hbm, residual_hbm,
    token_out, gate_out, down_out,
    ids_ref, probs_ref, tok_in, cot_in, gate_up, down, residual, gate_up_t, down_t,
    place, slot_weight, tok_send, grad_send, tok_relay, grad_relay,
    tok_all, grad_all, both, back, hidden, sum_gate, sum_down,
    tok_early, tok_late, hid_early, hid_late, tok_early_pair, tok_late_pair, hid_early_pair, hid_late_pair,
    grad_pair, back_pair, residual_pair,
    part, part_relay, returned,
    half_back, own, az_buf, ay_buf, by_buf, hub_buf, bz_buf, final, final_gate, final_down,
    load_sem, swap_sem, return_sem, pair_sem, az_sem, ay_sem, by_sem, hub_sem, bz_sem,
):
    bf16 = jnp.bfloat16
    me, x = lax.axis_index("dp"), lax.axis_index("expert")
    z, y, core = me // (CHIPS_Y * CORES), (me // CORES) % CHIPS_Y, me % CORES

    def at(zz, yy, cc):
        return (((zz + CHIPS_Z) % CHIPS_Z) * CHIPS_Y + (yy + CHIPS_Y) % CHIPS_Y) * CORES + cc

    def zi(off):
        return (z + off + CHIPS_Z) % CHIPS_Z

    def yi(off):
        return (y + off + CHIPS_Y) % CHIPS_Y

    partner = (at(z, y, 1 - core), x)
    z_side = ((at(z + 1, y, core), x), (at(z - 1, y, core), x))
    y_side = ((at(z, y + 1, core), x), (at(z, y - 1, core), x))
    x_side = ((me, (x + 1) % EXPERTS), (me, (x + EXPERTS - 1) % EXPERTS))
    barrier = pltpu.get_barrier_semaphore()
    z_far = [(at(z + off, y, core), x) for off in (2, -2)]
    y_far = [(at(z, y + 2, core), x)]
    for device in (partner, *z_side, *y_side, *x_side, *z_far, *y_far):
        pl.semaphore_signal(barrier, inc=1, device_id=device, device_id_type=MESH)

    loads = [
        pltpu.make_async_copy(source, target, load_sem.at[k])
        for k, (source, target) in enumerate(
            (
                (ids_hbm, ids_ref),
                (probs_hbm, probs_ref),
                (tokens_hbm, tok_in),
                (cotangent_hbm, cot_in),
                (down_hbm, down),
                (gate_up_hbm, gate_up),
                (residual_hbm, residual),
            )
        )
    ]
    for copy in loads:
        copy.start()

    started = []

    def send(src, dst, sems, index, device):
        copy = pltpu.make_async_remote_copy(
            src_ref=src, dst_ref=dst, send_sem=sems.at[(0, *index)], recv_sem=sems.at[(1, *index)],
            device_id=device, device_id_type=MESH,
        )
        copy.start()
        started.append(copy)
        return copy

    loads[0].wait()
    loads[1].wait()
    ids, probs = ids_ref[...], probs_ref[...]
    before = lax.broadcasted_iota(jnp.int32, (TOK, TOK), 0) < lax.broadcasted_iota(jnp.int32, (TOK, TOK), 1)
    before = jnp.where(before, 1.0, 0.0).astype(bf16)
    slots = wide(lax.broadcasted_iota(jnp.int32, (CAP, TOK), 0))
    for k in range(EXPERTS):
        expert = (x + k) % EXPERTS
        hits = ids == expert
        member = jnp.sum(jnp.where(hits, 1.0, 0.0), axis=0, keepdims=True)
        weight = jnp.sum(jnp.where(hits, probs, 0.0), axis=0, keepdims=True)
        index = dot(jnp.broadcast_to(member, (8, TOK)).astype(bf16), before)[0:1]
        chosen = jnp.where((slots == index) & (member > 0.5), 1.0, 0.0)
        rows = slice(k * CAP, (k + 1) * CAP)
        place[rows] = chosen.astype(bf16)
        slot_weight[rows] = jnp.broadcast_to(jnp.sum(chosen * weight, axis=1, keepdims=True), (CAP, TOK))

    def pick_tokens(k, target, rows):
        def body(n):
            cols = columns(n, 512)
            target[rows, cols] = dot(place[k * CAP : (k + 1) * CAP], tok_in[:, cols]).astype(bf16)
        loop(4, body)

    def pick_grads(k, target, rows):
        def body(n):
            cols = columns(n, 512)
            block = slice(k * CAP, (k + 1) * CAP)
            value = dot(place[block], cot_in[:, cols]) * slot_weight[block, 0:1]
            target[rows, cols] = value.astype(bf16)
        loop(4, body)

    swap = {}
    first, second, third = slice(0, CAP), slice(CAP, 2 * CAP), slice(2 * CAP, 3 * CAP)
    loads[2].wait()
    pick_tokens(2, tok_send, second)
    pl.semaphore_wait(barrier, 10)
    swap["tok", "leg"] = send(tok_send.at[second], tok_relay, swap_sem, (0,), x_side[0])
    loads[3].wait()
    pick_grads(2, grad_send, second)
    swap["grad", "leg"] = send(grad_send.at[second], grad_relay, swap_sem, (1,), x_side[1])
    pick_tokens(1, tok_send, first)
    left, right = slice(0, 1024), slice(1024, 2048)
    swap["tok", 0, 0] = send(tok_send.at[first, left], tok_all.at[LOW, left], swap_sem, (2,), x_side[0])
    pick_tokens(3, tok_send, third)
    swap["tok", 1, 0] = send(tok_send.at[third, left], tok_all.at[HIGH, left], swap_sem, (3,), x_side[1])
    pick_grads(1, grad_send, first)
    pick_grads(3, grad_send, third)
    pick_tokens(0, tok_all, SELF)
    pick_grads(0, grad_all, SELF)
    loads[4].wait()

    def turn_down(n):
        rows = columns(n, 256)
        down_t[rows, :] = down[:, rows].T

    loop(8, turn_down)
    swap["tok", "leg"].wait_recv()
    swap["tok", "far"] = send(tok_relay, tok_all.at[OPP], swap_sem, (4,), x_side[0])
    swap["grad", "leg"].wait_recv()
    swap["grad", "far"] = send(grad_relay, grad_all.at[OPP], swap_sem, (5,), x_side[1])
    swap["tok", 0, 1] = send(tok_send.at[first, right], tok_all.at[LOW, right], swap_sem, (10,), x_side[0])
    swap["tok", 1, 1] = send(tok_send.at[third, right], tok_all.at[HIGH, right], swap_sem, (11,), x_side[1])
    mine, theirs = columns(core, WIDTH), columns(1 - core, WIDTH)
    for part_at, cols in enumerate((theirs, mine)):
        swap["grad", 0, part_at] = send(
            grad_send.at[first, cols], grad_all.at[LOW, cols], swap_sem, (6 + part_at,), x_side[0]
        )
        swap["grad", 1, part_at] = send(
            grad_send.at[third, cols], grad_all.at[HIGH, cols], swap_sem, (8 + part_at,), x_side[1]
        )
    pair = {}

    def to_partner(name, index, src, dst):
        pair[name] = send(src, dst, pair_sem, (index,), partner)

    to_partner("grad self", 1, grad_all.at[SELF, theirs], grad_pair.at[SELF])
    loads[5].wait()

    def turn_gate_up(n):
        rows = columns(n, 256)
        gate_up_t[:, rows] = gate_up[rows, :].T

    loop(8, turn_gate_up)
    loads[6].wait()

    def project(rows):
        def body(n):
            cols = columns(n, 256)
            both[rows, cols] = dot(tok_all[rows], gate_up[:, cols])
        loop(4, body)

        def gates(n):
            r = pl.ds(pl.multiple_of(rows.start + n * 16, 16), 16)
            gate, up = both[r, 0:UNITS], both[r, UNITS : 2 * UNITS]
            sig = jax.nn.sigmoid(gate)
            active = gate * sig
            hidden[r] = (active * up).astype(bf16)
            both[r, 0:UNITS] = up * sig * (1.0 + gate * (1.0 - sig))
            both[r, UNITS : 2 * UNITS] = active
        loop((rows.stop - rows.start) // 16, gates)

    def pull_back(rows):
        def body(n):
            cols, upper = columns(n, 256), columns(n + 2, 256)
            value = dot(grad_all[rows], down_t[:, cols])
            back[rows, cols] = (value * both[rows, cols]).astype(bf16)
            back[rows, upper] = (value * both[rows, upper]).astype(bf16)
        loop(2, body)

    my_units, their_units = columns(core, HALF), columns(1 - core, HALF)
    to_partner("residual", 2, residual.at[:, theirs], residual_pair)
    def turn_tokens(rows, target):
        def body(n):
            cols = columns(n, 256)
            target[cols, :] = tok_all[rows, cols].T
        loop(8, body)

    def turn_hidden(rows, target):
        def body(n):
            cols = columns(n, 256)
            target[cols, :] = hidden[rows, cols].T
        loop(2, body)

    project(SELF)
    swap["tok", "far"].wait_recv()
    turn_tokens(EARLY, tok_early)
    to_partner("tok early", 4, tok_early, tok_early_pair)
    swap["grad", "far"].wait_recv()
    to_partner("grad far", 6, grad_all.at[OPP, theirs], grad_pair.at[OPP])
    project(OPP)
    turn_hidden(EARLY, hid_early)
    to_partner("hidden early", 5, hid_early, hid_early_pair)
    pull_back(EARLY)
    to_partner("back early", 7, back.at[EARLY, their_units], back_pair.at[EARLY])

    def down_columns(half):
        return pl.ds(pl.multiple_of(core * WIDTH + half * 512, 512), 512)

    for name in ("residual", "grad self", "grad far", "hidden early"):
        pair[name].wait_recv()

    def early_down(n):
        rows = columns(n, 128)
        for half in range(2):
            cols = slice(half * 512, half * 512 + 512)
            start = wide(residual[rows, down_columns(half)]) + wide(residual_pair[rows, cols])
            start = start + dot(hid_early[rows], grad_all[EARLY, down_columns(half)])
            sum_down[rows, cols] = start + dot(hid_early_pair[rows], grad_pair[EARLY, cols])
    loop(4, early_down)
    for name in ("tok early", "back early"):
        pair[name].wait_recv()

    def early_gate(n):
        rows = columns(n, 256)
        value = dot(tok_early[rows], back[EARLY, my_units])
        sum_gate[rows, :] = value + dot(tok_early_pair[rows], back_pair[EARLY])
    loop(8, early_gate)

    for part_at in range(2):
        for side in range(2):
            swap["tok", side, part_at].wait_recv()
    turn_tokens(LATE, tok_late)
    to_partner("tok late", 0, tok_late, tok_late_pair)
    project(LATE)
    turn_hidden(LATE, hid_late)
    to_partner("hidden late", 3, hid_late, hid_late_pair)
    swap["grad", 0, 0].wait_recv()
    to_partner("grad low", 9, grad_all.at[LOW, theirs], grad_pair.at[LOW])
    swap["grad", 1, 0].wait_recv()
    to_partner("grad high", 10, grad_all.at[HIGH, theirs], grad_pair.at[HIGH])

    def half_pull(n):
        cols = columns(n, 256)
        half_back[:, cols] = dot(grad_all[LATE, theirs], down_t[theirs, cols])
    loop(2, half_pull)
    swap["grad", 0, 1].wait_recv()
    swap["grad", 1, 1].wait_recv()

    def late_pull(n):
        cols, upper = columns(n, 256), columns(n + 2, 256)
        value = half_back[:, cols] + dot(grad_all[LATE, mine], down_t[mine, cols])
        back[LATE, cols] = (value * both[LATE, cols]).astype(bf16)
        back[LATE, upper] = (value * both[LATE, upper]).astype(bf16)
    loop(2, late_pull)
    to_partner("back late", 11, back.at[LATE, their_units], back_pair.at[LATE])
    def late_gate(n):
        rows = columns(n, 256)
        sum_gate[rows, :] += dot(tok_late[rows], back[LATE, my_units])
    loop(8, late_gate)
    for name in ("grad low", "grad high", "hidden late"):
        pair[name].wait_recv()

    def late_down(n):
        rows = columns(n, 128)
        for half in range(2):
            cols = slice(half * 512, half * 512 + 512)
            value = dot(hid_late[rows], grad_all[LATE, down_columns(half)])
            sum_down[rows, cols] += value + dot(hid_late_pair[rows], grad_pair[LATE, cols])
    loop(4, late_down)
    for name in ("tok late", "back late"):
        pair[name].wait_recv()

    def group(off):
        zz = zi(off)
        rows = columns(zz, 256)
        value = sum_gate[rows, :] + dot(tok_late_pair[rows], back_pair[LATE])
        for yy in range(CHIPS_Y):
            down_rows = pl.ds(pl.multiple_of(zz * 64 + yy * 16, 16), 16)
            own[zz, yy, 0:64] = value[64 * yy : 64 * yy + 64].astype(bf16)
            own[zz, yy, 64:80] = sum_down[down_rows, 0:512].astype(bf16)
            own[zz, yy, 80:96] = sum_down[down_rows, 512:1024].astype(bf16)

    back_copies = {}

    def token_columns(n):
        cols = slice(n * 256, n * 256 + 256)
        value = dot(back[...], gate_up_t[:, cols]).astype(bf16)
        part[:, cols] = value
        returned[0:CAP, cols] = value[SELF]

    def give_back(half):
        cols = slice(half * 1024, half * 1024 + 1024)
        other = x_side[half]
        back_copies["high", half] = send(
            part.at[HIGH, cols], returned.at[3 * CAP : 4 * CAP, cols], return_sem, (half, 0), x_side[0]
        )
        back_copies["low", half] = send(
            part.at[LOW, cols], returned.at[CAP : 2 * CAP, cols], return_sem, (half, 1), x_side[1]
        )
        back_copies["leg", half] = send(
            part.at[OPP, cols], part_relay.at[half], return_sem, (half, 2), other
        )

    def pass_on(half):
        cols = slice(half * 1024, half * 1024 + 1024)
        back_copies["leg", half].wait_recv()
        back_copies["far", half] = send(
            part_relay.at[half], returned.at[2 * CAP : 3 * CAP, cols], return_sem, (half, 3), x_side[half]
        )

    def combine():
        for half in range(2):
            for name in ("high", "low", "far"):
                back_copies[name, half].wait_recv()

        def body(n):
            cols = columns(n, 256)
            token_out[:, cols] = dot_rows(place[...], returned[:, cols]).astype(bf16)
        loop(8, body)

    rows_a, rows_b = slice(0, ROWS_A), slice(ROWS_A, SHARE)
    copies = {}

    def add_into(zz, yy, rows, arrived):
        own[zz, yy, rows] = (wide(own[zz, yy, rows]) + wide(arrived)).astype(bf16)

    def a_z(side, step, off_y):
        off = (5 - step) if side == 0 else step - 5
        slot = ORDER_Y.index(off_y)
        if ("az", side, step - 1, off_y) in copies:
            copies["az", side, step - 1, off_y].wait_recv()
            add_into(zi(off), yi(off_y), rows_a, az_buf[side, step - 2, slot])
        copies["az", side, step, off_y] = send(
            own.at[zi(off), yi(off_y), rows_a], az_buf.at[side, step - 1, slot], az_sem,
            (side, step - 1, slot), z_side[side],
        )

    def a_z_end(off_y):
        slot = ORDER_Y.index(off_y)
        total = wide(own[z, yi(off_y), rows_a])
        for side in range(2):
            copies["az", side, 4, off_y].wait_recv()
            total = total + wide(az_buf[side, 3, slot])
        if off_y == 0:
            return total
        own[z, yi(off_y), rows_a] = total.astype(bf16)
        copies["ay", off_y] = send(
            own.at[z, yi(off_y), rows_a], ay_buf.at[slot], ay_sem, (slot,), (at(z, y + off_y, core), x)
        )

    def finish(total, rows):
        final[rows] = total * (1.0 / (CHIPS_Z * CHIPS_Y * CORES))

    def a_end(total):
        for off_y in (2, 1, -1):
            copies["ay", off_y].wait_recv()
            total = total + wide(ay_buf[ORDER_Y.index(off_y)])
        finish(total, rows_a)

    def b_y(side, step, piece):
        off = (3 - step) if side == 0 else step - 3
        slot = GROUPS.index(piece)
        if ("by", side, step - 1, piece) in copies:
            copies["by", side, step - 1, piece].wait_recv()
            add_into(zi(piece), yi(off), rows_b, by_buf[side, step - 2, slot])
        copies["by", side, step, piece] = send(
            own.at[zi(piece), yi(off), rows_b], by_buf.at[side, step - 1, slot], by_sem,
            (side, step - 1, slot), y_side[side],
        )

    def b_y_end(piece):
        slot = GROUPS.index(piece)
        total = wide(own[zi(piece), y, rows_b])
        for side in range(2):
            copies["by", side, 2, piece].wait_recv()
            total = total + wide(by_buf[side, 1, slot])
        if piece == 0:
            return total
        src = own.at[zi(piece), y]
        src[rows_b] = total.astype(bf16)
        if piece == 4:
            for side, (lo, hi) in enumerate(FAR_PARTS):
                copies["far", side] = send(
                    src.at[ROWS_A + lo : ROWS_A + hi], hub_buf.at[side, 0, lo:hi], hub_sem, (side, 0),
                    (at(z + (2, -2)[side], y, core), x),
                )
        elif abs(piece) == 3:
            side = 0 if piece > 0 else 1
            copies["near", side] = send(src.at[rows_b], hub_buf.at[side, 1], hub_sem, (side, 1), z_side[side])
        elif abs(piece) == 2:
            side = 0 if piece > 0 else 1
            lo, hi = FAR_PARTS[side]
            copies["far", side].wait_recv()
            copies["near", side].wait_recv()
            part_rows = slice(ROWS_A + lo, ROWS_A + hi)
            src[rows_b] = (wide(src[rows_b]) + wide(hub_buf[side, 1])).astype(bf16)
            src[part_rows] = (wide(src[part_rows]) + wide(hub_buf[side, 0, lo:hi])).astype(bf16)
            copies["bz", piece] = send(
                src.at[rows_b], bz_buf.at[side], bz_sem, (side,), (at(z + piece, y, core), x)
            )
        else:
            side = 0 if piece > 0 else 1
            copies["bz", piece] = send(src.at[rows_b], bz_buf.at[2 + side], bz_sem, (2 + side,), z_side[side])

    def b_end(total):
        for slot, piece in enumerate((2, -2, 1, -1)):
            copies["bz", piece].wait_recv()
            total = total + wide(bz_buf[slot])
        finish(total, rows_b)

    def final_swap():
        other = 1 - core
        gate_rows = pl.ds(pl.multiple_of(32 * other, 32), 32)
        last = [send(final.at[gate_rows], final_gate, bz_sem, (4,), partner)]
        for k in range(2):
            down_rows = pl.ds(pl.multiple_of(64 + 16 * k + 8 * other, 8), 8)
            last.append(send(final.at[down_rows], final_down.at[k], bz_sem, (5 + k,), partner))
        gate_out[:, my_units] = final[pl.ds(pl.multiple_of(32 * core, 32), 32)]
        for k in range(2):
            down_out[:, down_columns(k)] = final[pl.ds(pl.multiple_of(64 + 16 * k + 8 * core, 8), 8)]
        for copy in last:
            copy.wait_recv()
        gate_out[:, their_units] = final_gate[...]
        for k in range(2):
            cols = pl.ds(pl.multiple_of(other * WIDTH + k * 512, 512), 512)
            down_out[:, cols] = final_down[k]

    upper = (4, 3, 2, 1)
    edge = {0: (2, 1), 1: (-1, 0)}

    def b_start(piece):
        far = 0 if piece in upper else 1
        b_y(far, 1, piece)
        b_y(1 - far, 2, piece)

    def b_next(piece):
        b_y(0 if piece in upper else 1, 2, piece)

    def a_step(step, own_edge):
        for k in range(2):
            for side in range(2):
                a_z(side, step, edge[side if own_edge else 1 - side][k])

    group(4)
    a_step(1, True)
    b_start(4)
    group(-3)
    for off_y in edge[0]:
        a_z(1, 2, off_y)
    group(3)
    for off_y in edge[1]:
        a_z(0, 2, off_y)
    b_start(-3)
    b_start(3)
    for off in GROUPS[3:]:
        group(off)
        if off in (-2, 2):
            b_start(off)
    for n in range(4):
        token_columns(n)
    give_back(0)
    a_step(2, True)
    b_start(-1)
    token_columns(4)
    b_next(4)
    b_start(1)
    a_step(3, False)
    b_next(-3)
    token_columns(5)
    b_next(3)
    b_start(0)
    token_columns(6)
    a_step(3, True)
    b_next(-2)
    b_y_end(4)
    token_columns(7)
    give_back(1)
    b_next(2)
    b_y_end(-3)
    a_step(4, False)
    b_y_end(3)
    b_next(-1)
    b_next(1)
    b_y_end(-2)
    a_step(4, True)
    b_next(0)
    b_y_end(2)
    pass_on(0)
    b_y_end(-1)
    a_z_end(2)
    a_z_end(-1)
    b_y_end(1)
    a_z_end(1)
    total_b = b_y_end(0)
    total_a = a_z_end(0)
    pass_on(1)
    final[rows_a], final[rows_b] = total_a, total_b
    combine()
    a_end(final[rows_a])
    b_end(final[rows_b])
    final_swap()
    for copy in started:
        copy.wait_send()


def store_kernel(*refs):
    sources, targets, sems = refs[:3], refs[3:6], refs[6]
    stores = [pltpu.make_async_copy(sources[k], targets[k], sems.at[k]) for k in range(3)]
    for copy in stores:
        copy.start()
    for copy in stores:
        copy.wait()


def on_device(
    tokens, cotangent, expert_ids, gate_probs, gate_up_weight, down_weight, down_residual
):
    bf16, f32 = jnp.bfloat16, jnp.float32
    sems = pltpu.SemaphoreType.DMA
    vmem, anywhere = pl.BlockSpec(memory_space=pltpu.VMEM), pl.BlockSpec(memory_space=pl.ANY)
    shapes = (
        ((2, TOK), jnp.int32), ((2, TOK), f32),
        ((TOK, MODEL), bf16), ((TOK, MODEL), bf16), ((MODEL, WIDTH), bf16), ((UNITS, MODEL), bf16),
        ((UNITS, MODEL), bf16), ((WIDTH, MODEL), bf16), ((MODEL, UNITS), bf16),
        ((ROWS, TOK), bf16), ((ROWS, TOK), f32), ((3 * CAP, MODEL), bf16), ((3 * CAP, MODEL), bf16),
        ((CAP, MODEL), bf16), ((CAP, MODEL), bf16),
        ((ROWS, MODEL), bf16), ((ROWS, MODEL), bf16), ((ROWS, WIDTH), f32), ((ROWS, WIDTH), bf16),
        ((ROWS, UNITS), bf16), ((MODEL, HALF), f32), ((UNITS, WIDTH), f32),
        *(2 * (((MODEL, 2 * CAP), bf16), ((MODEL, 2 * CAP), bf16), ((UNITS, 2 * CAP), bf16), ((UNITS, 2 * CAP), bf16))),
        ((ROWS, WIDTH), bf16), ((ROWS, HALF), bf16), ((UNITS, WIDTH), bf16),
        ((ROWS, MODEL), bf16), ((2, CAP, MODEL // 2), bf16), ((ROWS, MODEL), bf16),
        ((2 * CAP, UNITS), f32), ((CHIPS_Z, CHIPS_Y, SHARE, HALF), bf16),
        ((2, 4, CHIPS_Y, ROWS_A, HALF), bf16), ((3, ROWS_A, HALF), bf16),
        ((2, 2, CHIPS_Z, ROWS_B, HALF), bf16), ((2, 2, ROWS_B, HALF), bf16), ((4, ROWS_B, HALF), bf16),
        ((SHARE, HALF), f32), ((GATE_ROWS, HALF), f32), ((2, DOWN_ROWS, HALF), f32),
    )
    semaphores = ((7,), (2, 12), (2, 2, 4), (2, 12), (2, 2, 4, 4), (2, 3), (2, 2, 2, 8), (2, 2, 2), (2, 7))
    results = (
        jax.ShapeDtypeStruct((TOK, MODEL), bf16),
        jax.ShapeDtypeStruct((GATE_ROWS, WIDTH), f32),
        jax.ShapeDtypeStruct((DOWN_ROWS, MODEL), f32),
    )
    values = pl.pallas_call(
        layer_kernel,
        out_shape=results,
        in_specs=[pl.BlockSpec(memory_space=pltpu.HBM)] * 7,
        out_specs=(vmem, vmem, vmem),
        scratch_shapes=[pltpu.VMEM(*shape) for shape in shapes] + [sems(shape) for shape in semaphores],
        compiler_params=pltpu.CompilerParams(
            collective_id=0, has_side_effects=True, vmem_limit_bytes=53 * 1024 * 1024
        ),
    )(
        expert_ids.T, gate_probs.T, tokens, cotangent, gate_up_weight[0], down_weight[0], down_residual[0, 0]
    )
    token_grad, gate_up_part, down_part = pl.pallas_call(
        store_kernel,
        out_shape=results,
        in_specs=[anywhere] * 3,
        out_specs=(anywhere,) * 3,
        scratch_shapes=[sems((3,))],
        compiler_params=pltpu.CompilerParams(vmem_limit_bytes=1024 * 1024),
    )(*values)
    return (token_grad, gate_up_part[None], down_part[None])


def solution(mesh):
    placed = (
        P(("dp", "expert"), None),
        P(("dp", "expert"), None),
        P(("dp", "expert"), None),
        P(("dp", "expert"), None),
        P("expert", None, None),
        P("expert", None, None),
        P("dp", "expert", None, None),
    )
    return jax.shard_map(
        on_device,
        mesh=mesh,
        in_specs=placed,
        out_specs=(P(("dp", "expert"), None), P("expert", "dp", None), P("expert", "dp", None)),
        check_vma=False,
    )
```

```python
import jax
import jax.numpy as jnp
from jax import lax
from jax.experimental import pallas as pl
from jax.experimental.pallas import tpu as pltpu
from jax.sharding import PartitionSpec as P

MESH = pl.DeviceIdType.MESH
CHIPS_Z, CHIPS_Y, CORES, EXPERTS = 8, 4, 2, 4
SHARE, WIDTH, HALF = 96, 1024, 512
GATE_ROWS, DOWN_ROWS = 32, 8
ROWS_A = 48
ROWS_B = SHARE - ROWS_A
FAR_PARTS = ((0, 32), (32, ROWS_B))
GROUPS = (4, -3, 3, -2, 2, -1, 1, 0)
ORDER_Y = (2, 1, -1, 0)
TOK, CAP, MODEL, UNITS = 128, 80, 2048, 512
ROWS = EXPERTS * CAP
OPP, SELF, LOW, HIGH = (slice(k * CAP, (k + 1) * CAP) for k in range(4))
EARLY, LATE, NEAR = slice(0, 2 * CAP), slice(2 * CAP, ROWS), slice(CAP, ROWS)


def wide(value):
    return value.astype(jnp.float32)


def dot(left, right):
    return jnp.dot(left, right, preferred_element_type=jnp.float32)


def dot_rows(left, right):
    return lax.dot_general(left, right, (((0,), (0,)), ((), ())), preferred_element_type=jnp.float32)


def columns(index, width):
    return pl.ds(pl.multiple_of(index * width, width), width)


def loop(count, body):
    def step(index, carry):
        body(index)
        return carry

    lax.fori_loop(0, count, step, 0)


def layer_kernel(
    ids_hbm, probs_hbm, tokens_hbm, cotangent_hbm, gate_up_hbm, down_hbm, residual_hbm,
    token_out, gate_out, down_out,
    ids_ref, probs_ref, tok_in, cot_in, gate_up, down, residual, gate_up_t, down_t,
    place, place_t, slot_weight, tok_send, grad_send, tok_relay, grad_relay,
    tok_all, grad_all, both, back, hidden, sum_gate, sum_down,
    tok_early, tok_late, hid_early, hid_late, tok_early_pair, tok_late_pair, hid_early_pair, hid_late_pair,
    grad_pair, back_pair, residual_pair,
    part, part_relay, returned,
    half_back, own, az_buf, ay_buf, by_buf, hub_buf, bz_buf, final, final_pair,
    load_sem, swap_sem, return_sem, pair_sem, az_sem, ay_sem, by_sem, hub_sem, bz_sem,
):
    bf16 = jnp.bfloat16
    me, x = lax.axis_index("dp"), lax.axis_index("expert")
    z, y, core = me // (CHIPS_Y * CORES), (me // CORES) % CHIPS_Y, me % CORES

    def at(zz, yy, cc):
        return (((zz + CHIPS_Z) % CHIPS_Z) * CHIPS_Y + (yy + CHIPS_Y) % CHIPS_Y) * CORES + cc

    def zi(off):
        return (z + off + CHIPS_Z) % CHIPS_Z

    def yi(off):
        return (y + off + CHIPS_Y) % CHIPS_Y

    partner = (at(z, y, 1 - core), x)
    z_side = ((at(z + 1, y, core), x), (at(z - 1, y, core), x))
    y_side = ((at(z, y + 1, core), x), (at(z, y - 1, core), x))
    x_side = ((me, (x + 1) % EXPERTS), (me, (x + EXPERTS - 1) % EXPERTS))
    barrier = pltpu.get_barrier_semaphore()
    z_far = [(at(z + off, y, core), x) for off in (2, -2)]
    y_far = [(at(z, y + 2, core), x)]
    for device in (partner, *z_side, *y_side, *x_side, *z_far, *y_far):
        pl.semaphore_signal(barrier, inc=1, device_id=device, device_id_type=MESH)

    loads = [
        pltpu.make_async_copy(source, target, load_sem.at[k])
        for k, (source, target) in enumerate(
            (
                (ids_hbm, ids_ref),
                (probs_hbm, probs_ref),
                (tokens_hbm, tok_in),
                (cotangent_hbm, cot_in),
                (down_hbm, down),
                (gate_up_hbm, gate_up),
                (residual_hbm, residual),
            )
        )
    ]
    for copy in loads:
        copy.start()

    started = []

    def send(src, dst, sems, index, device):
        copy = pltpu.make_async_remote_copy(
            src_ref=src, dst_ref=dst, send_sem=sems.at[(0, *index)], recv_sem=sems.at[(1, *index)],
            device_id=device, device_id_type=MESH,
        )
        copy.start()
        started.append(copy)
        return copy

    loads[0].wait()
    loads[1].wait()
    ids, probs = ids_ref[...], probs_ref[...]
    before = lax.broadcasted_iota(jnp.int32, (TOK, TOK), 0) < lax.broadcasted_iota(jnp.int32, (TOK, TOK), 1)
    before = jnp.where(before, 1.0, 0.0).astype(bf16)
    slots = wide(lax.broadcasted_iota(jnp.int32, (CAP, TOK), 0))
    for k in range(EXPERTS):
        expert = (x + k) % EXPERTS
        hits = ids == expert
        member = jnp.sum(jnp.where(hits, 1.0, 0.0), axis=0, keepdims=True)
        weight = jnp.sum(jnp.where(hits, probs, 0.0), axis=0, keepdims=True)
        index = dot(jnp.broadcast_to(member, (8, TOK)).astype(bf16), before)[0:1]
        chosen = jnp.where((slots == index) & (member > 0.5), 1.0, 0.0)
        rows = slice(k * CAP, (k + 1) * CAP)
        place[rows] = chosen.astype(bf16)
        slot_weight[rows] = jnp.broadcast_to(jnp.sum(chosen * weight, axis=1, keepdims=True), (CAP, TOK))

    def pick_tokens(k, target, rows):
        def body(n):
            cols = columns(n, 512)
            target[rows, cols] = dot(place[k * CAP : (k + 1) * CAP], tok_in[:, cols]).astype(bf16)
        loop(4, body)

    def pick_grads(k, target, rows):
        def body(n):
            cols = columns(n, 512)
            block = slice(k * CAP, (k + 1) * CAP)
            value = dot(place[block], cot_in[:, cols]) * slot_weight[block, 0:1]
            target[rows, cols] = value.astype(bf16)
        loop(4, body)

    swap = {}
    first, second, third = slice(0, CAP), slice(CAP, 2 * CAP), slice(2 * CAP, 3 * CAP)
    loads[2].wait()
    pick_tokens(2, tok_send, second)
    pl.semaphore_wait(barrier, 10)
    swap["tok", "leg"] = send(tok_send.at[second], tok_relay, swap_sem, (0,), x_side[0])
    loads[3].wait()
    pick_grads(2, grad_send, second)
    swap["grad", "leg"] = send(grad_send.at[second], grad_relay, swap_sem, (1,), x_side[1])
    pick_tokens(1, tok_send, first)
    left, right = slice(0, 1024), slice(1024, 2048)
    swap["tok", 0, 0] = send(tok_send.at[first, left], tok_all.at[LOW, left], swap_sem, (2,), x_side[0])
    pick_tokens(3, tok_send, third)
    swap["tok", 1, 0] = send(tok_send.at[third, left], tok_all.at[HIGH, left], swap_sem, (3,), x_side[1])
    pick_grads(1, grad_send, first)
    pick_grads(3, grad_send, third)
    pick_tokens(0, tok_all, SELF)
    pick_grads(0, grad_all, SELF)
    loads[4].wait()

    def turn_down(n):
        rows = columns(n, 256)
        down_t[rows, :] = down[:, rows].T

    loop(8, turn_down)
    swap["tok", "leg"].wait_recv()
    swap["tok", "far"] = send(tok_relay, tok_all.at[OPP], swap_sem, (4,), x_side[0])
    swap["grad", "leg"].wait_recv()
    swap["grad", "far"] = send(grad_relay, grad_all.at[OPP], swap_sem, (5,), x_side[1])
    swap["tok", 0, 1] = send(tok_send.at[first, right], tok_all.at[LOW, right], swap_sem, (10,), x_side[0])
    swap["tok", 1, 1] = send(tok_send.at[third, right], tok_all.at[HIGH, right], swap_sem, (11,), x_side[1])
    mine, theirs = columns(core, WIDTH), columns(1 - core, WIDTH)
    for part_at, cols in enumerate((theirs, mine)):
        swap["grad", 0, part_at] = send(
            grad_send.at[first, cols], grad_all.at[LOW, cols], swap_sem, (6 + part_at,), x_side[0]
        )
        swap["grad", 1, part_at] = send(
            grad_send.at[third, cols], grad_all.at[HIGH, cols], swap_sem, (8 + part_at,), x_side[1]
        )
    pair = {}

    def to_partner(name, index, src, dst):
        pair[name] = send(src, dst, pair_sem, (index,), partner)

    to_partner("grad self", 1, grad_all.at[SELF, theirs], grad_pair.at[SELF])
    loads[5].wait()

    def turn_gate_up(n):
        rows = columns(n, 256)
        gate_up_t[:, rows] = gate_up[rows, :].T

    loop(8, turn_gate_up)
    place_t[...] = place[...].T
    loads[6].wait()

    def project(rows):
        def body(n):
            cols = columns(n, 256)
            both[rows, cols] = dot(tok_all[rows], gate_up[:, cols])
        loop(4, body)

        def gates(n):
            r = pl.ds(pl.multiple_of(rows.start + n * 16, 16), 16)
            gate, up = both[r, 0:UNITS], both[r, UNITS : 2 * UNITS]
            sig = jax.nn.sigmoid(gate)
            active = gate * sig
            hidden[r] = (active * up).astype(bf16)
            both[r, 0:UNITS] = up * sig * (1.0 + gate * (1.0 - sig))
            both[r, UNITS : 2 * UNITS] = active
        loop((rows.stop - rows.start) // 16, gates)

    def pull_back(rows):
        def body(n):
            cols, upper = columns(n, 256), columns(n + 2, 256)
            value = dot(grad_all[rows], down_t[:, cols])
            back[rows, cols] = (value * both[rows, cols]).astype(bf16)
            back[rows, upper] = (value * both[rows, upper]).astype(bf16)
        loop(2, body)

    my_units, their_units = columns(core, HALF), columns(1 - core, HALF)
    to_partner("residual", 2, residual.at[:, theirs], residual_pair)
    def turn_tokens(rows, target):
        def body(n):
            cols = columns(n, 256)
            target[cols, :] = tok_all[rows, cols].T
        loop(8, body)

    def turn_hidden(rows, target):
        def body(n):
            cols = columns(n, 256)
            target[cols, :] = hidden[rows, cols].T
        loop(2, body)

    project(SELF)
    swap["tok", "far"].wait_recv()
    turn_tokens(EARLY, tok_early)
    to_partner("tok early", 4, tok_early, tok_early_pair)
    swap["grad", "far"].wait_recv()
    to_partner("grad far", 6, grad_all.at[OPP, theirs], grad_pair.at[OPP])
    project(OPP)
    turn_hidden(EARLY, hid_early)
    to_partner("hidden early", 5, hid_early, hid_early_pair)
    pull_back(EARLY)
    to_partner("back early", 7, back.at[EARLY, their_units], back_pair.at[EARLY])

    for part_at in range(2):
        for side in range(2):
            swap["tok", side, part_at].wait_recv()
    turn_tokens(LATE, tok_late)
    to_partner("tok late", 0, tok_late, tok_late_pair)
    project(LATE)
    turn_hidden(LATE, hid_late)
    to_partner("hidden late", 3, hid_late, hid_late_pair)
    def down_columns(half):
        return pl.ds(pl.multiple_of(core * WIDTH + half * 512, 512), 512)

    for name in ("residual", "grad self", "grad far", "hidden early"):
        pair[name].wait_recv()

    def early_down(n):
        rows = columns(n, 128)
        for half in range(2):
            cols = slice(half * 512, half * 512 + 512)
            start = wide(residual[rows, down_columns(half)]) + wide(residual_pair[rows, cols])
            start = start + dot(hid_early[rows], grad_all[EARLY, down_columns(half)])
            sum_down[rows, cols] = start + dot(hid_early_pair[rows], grad_pair[EARLY, cols])
    loop(4, early_down)
    for name in ("tok early", "back early"):
        pair[name].wait_recv()

    def early_gate(n):
        rows = columns(n, 256)
        value = dot(tok_early[rows], back[EARLY, my_units])
        sum_gate[rows, :] = value + dot(tok_early_pair[rows], back_pair[EARLY])
    loop(8, early_gate)

    swap["grad", 0, 0].wait_recv()
    to_partner("grad low", 9, grad_all.at[LOW, theirs], grad_pair.at[LOW])
    swap["grad", 1, 0].wait_recv()
    to_partner("grad high", 10, grad_all.at[HIGH, theirs], grad_pair.at[HIGH])

    def half_pull(n):
        cols = columns(n, 256)
        half_back[:, cols] = dot(grad_all[LATE, theirs], down_t[theirs, cols])
    loop(2, half_pull)
    swap["grad", 0, 1].wait_recv()
    swap["grad", 1, 1].wait_recv()

    def late_pull(n):
        cols, upper = columns(n, 256), columns(n + 2, 256)
        value = half_back[:, cols] + dot(grad_all[LATE, mine], down_t[mine, cols])
        back[LATE, cols] = (value * both[LATE, cols]).astype(bf16)
        back[LATE, upper] = (value * both[LATE, upper]).astype(bf16)
    loop(2, late_pull)
    to_partner("back late", 11, back.at[LATE, their_units], back_pair.at[LATE])
    def late_gate(n):
        rows = columns(n, 256)
        sum_gate[rows, :] += dot(tok_late[rows], back[LATE, my_units])
    loop(8, late_gate)
    for name in ("grad low", "grad high", "hidden late"):
        pair[name].wait_recv()

    def late_down(n):
        rows = columns(n, 128)
        for half in range(2):
            cols = slice(half * 512, half * 512 + 512)
            value = dot(hid_late[rows], grad_all[LATE, down_columns(half)])
            sum_down[rows, cols] += value + dot(hid_late_pair[rows], grad_pair[LATE, cols])
    loop(4, late_down)
    for name in ("tok late", "back late"):
        pair[name].wait_recv()

    def group(off):
        zz = zi(off)
        rows = columns(zz, 256)
        value = sum_gate[rows, :] + dot(tok_late_pair[rows], back_pair[LATE])
        for yy in range(CHIPS_Y):
            down_rows = pl.ds(pl.multiple_of(zz * 64 + yy * 16, 16), 16)
            own[zz, yy, 0:64] = value[64 * yy : 64 * yy + 64].astype(bf16)
            own[zz, yy, 64:80] = sum_down[down_rows, 0:512].astype(bf16)
            own[zz, yy, 80:96] = sum_down[down_rows, 512:1024].astype(bf16)

    back_copies = {}

    def token_columns(n):
        cols = slice(n * 256, n * 256 + 256)
        value = dot(back[...], gate_up_t[:, cols]).astype(bf16)
        part[:, cols] = value
        returned[0:CAP, cols] = value[SELF]

    def give_back(half):
        cols = slice(half * 1024, half * 1024 + 1024)
        other = x_side[half]
        back_copies["leg", half] = send(
            part.at[OPP, cols], part_relay.at[half], return_sem, (half, 2), other
        )
        back_copies["high", half] = send(
            part.at[HIGH, cols], returned.at[3 * CAP : 4 * CAP, cols], return_sem, (half, 0), x_side[0]
        )
        back_copies["low", half] = send(
            part.at[LOW, cols], returned.at[CAP : 2 * CAP, cols], return_sem, (half, 1), x_side[1]
        )

    def pass_on(half):
        cols = slice(half * 1024, half * 1024 + 1024)
        back_copies["leg", half].wait_recv()
        back_copies["far", half] = send(
            part_relay.at[half], returned.at[2 * CAP : 3 * CAP, cols], return_sem, (half, 3), x_side[half]
        )

    def combine(half):
        for name in ("high", "low", "far"):
            back_copies[name, half].wait_recv()

        def body(n):
            cols = columns(n + 4 * half, 256)
            token_out[:, cols] = dot(place_t[...], returned[:, cols]).astype(bf16)
        loop(4, body)

    rows_a, rows_b = slice(0, ROWS_A), slice(ROWS_A, SHARE)
    copies = {}

    def add_into(zz, yy, rows, arrived):
        own[zz, yy, rows] = (wide(own[zz, yy, rows]) + wide(arrived)).astype(bf16)

    def a_z(side, step, off_y):
        off = (5 - step) if side == 0 else step - 5
        slot = ORDER_Y.index(off_y)
        if ("az", side, step - 1, off_y) in copies:
            copies["az", side, step - 1, off_y].wait_recv()
            add_into(zi(off), yi(off_y), rows_a, az_buf[side, step - 2, slot])
        copies["az", side, step, off_y] = send(
            own.at[zi(off), yi(off_y), rows_a], az_buf.at[side, step - 1, slot], az_sem,
            (side, step - 1, slot), z_side[side],
        )

    def a_z_end(off_y):
        slot = ORDER_Y.index(off_y)
        total = wide(own[z, yi(off_y), rows_a])
        for side in range(2):
            copies["az", side, 4, off_y].wait_recv()
            total = total + wide(az_buf[side, 3, slot])
        if off_y == 0:
            return total
        own[z, yi(off_y), rows_a] = total.astype(bf16)
        copies["ay", off_y] = send(
            own.at[z, yi(off_y), rows_a], ay_buf.at[slot], ay_sem, (slot,), (at(z, y + off_y, core), x)
        )

    def finish(total, rows):
        final[rows] = total * (1.0 / (CHIPS_Z * CHIPS_Y * CORES))

    def a_end(total):
        for off_y in (2, 1, -1):
            copies["ay", off_y].wait_recv()
            total = total + wide(ay_buf[ORDER_Y.index(off_y)])
        finish(total, rows_a)

    def b_y(side, step, piece):
        off = (3 - step) if side == 0 else step - 3
        slot = GROUPS.index(piece)
        if ("by", side, step - 1, piece) in copies:
            copies["by", side, step - 1, piece].wait_recv()
            add_into(zi(piece), yi(off), rows_b, by_buf[side, step - 2, slot])
        copies["by", side, step, piece] = send(
            own.at[zi(piece), yi(off), rows_b], by_buf.at[side, step - 1, slot], by_sem,
            (side, step - 1, slot), y_side[side],
        )

    def b_y_end(piece):
        slot = GROUPS.index(piece)
        total = wide(own[zi(piece), y, rows_b])
        for side in range(2):
            copies["by", side, 2, piece].wait_recv()
            total = total + wide(by_buf[side, 1, slot])
        if piece == 0:
            return total
        src = own.at[zi(piece), y]
        src[rows_b] = total.astype(bf16)
        if piece == 4:
            for side, (lo, hi) in enumerate(FAR_PARTS):
                copies["far", side] = send(
                    src.at[ROWS_A + lo : ROWS_A + hi], hub_buf.at[side, 0, lo:hi], hub_sem, (side, 0),
                    (at(z + (2, -2)[side], y, core), x),
                )
        elif abs(piece) == 3:
            side = 0 if piece > 0 else 1
            copies["near", side] = send(src.at[rows_b], hub_buf.at[side, 1], hub_sem, (side, 1), z_side[side])
        elif abs(piece) == 2:
            side = 0 if piece > 0 else 1
            lo, hi = FAR_PARTS[side]
            copies["far", side].wait_recv()
            copies["near", side].wait_recv()
            part_rows = slice(ROWS_A + lo, ROWS_A + hi)
            src[rows_b] = (wide(src[rows_b]) + wide(hub_buf[side, 1])).astype(bf16)
            src[part_rows] = (wide(src[part_rows]) + wide(hub_buf[side, 0, lo:hi])).astype(bf16)
            copies["bz", piece] = send(
                src.at[rows_b], bz_buf.at[side], bz_sem, (side,), (at(z + piece, y, core), x)
            )
        else:
            side = 0 if piece > 0 else 1
            copies["bz", piece] = send(src.at[rows_b], bz_buf.at[2 + side], bz_sem, (2 + side,), z_side[side])

    def b_end(total):
        for slot, piece in enumerate((2, -2, 1, -1)):
            copies["bz", piece].wait_recv()
            total = total + wide(bz_buf[slot])
        finish(total, rows_b)

    def to_other_core(rows, index):
        return send(final.at[rows], final_pair.at[rows], bz_sem, (4 + index,), partner)

    def store_shares():
        for source, units, first_col in ((final, my_units, core * WIDTH), (final_pair, their_units, (1 - core) * WIDTH)):
            gate_out[:, units] = source[pl.ds(pl.multiple_of(32 * core, 32), 32)]
            for k in range(2):
                cols = pl.ds(pl.multiple_of(first_col + k * 512, 512), 512)
                down_out[:, cols] = source[pl.ds(pl.multiple_of(64 + 16 * k + 8 * core, 8), 8)]

    upper = (4, 3, 2, 1)
    edge = {0: (2, 1), 1: (-1, 0)}

    def b_start(piece):
        far = 0 if piece in upper else 1
        b_y(far, 1, piece)
        b_y(1 - far, 2, piece)

    def b_next(piece):
        b_y(0 if piece in upper else 1, 2, piece)

    def a_step(step, own_edge):
        for k in range(2):
            for side in range(2):
                a_z(side, step, edge[side if own_edge else 1 - side][k])

    group(4)
    a_step(1, True)
    b_start(4)
    group(-3)
    for off_y in edge[0]:
        a_z(1, 2, off_y)
    group(3)
    for off_y in edge[1]:
        a_z(0, 2, off_y)
    b_start(-3)
    b_start(3)
    for off in GROUPS[3:]:
        group(off)
        if off in (-2, 2):
            b_start(off)
    for n in range(4):
        token_columns(n)
    give_back(0)
    token_columns(4)
    a_step(2, True)
    b_start(-1)
    token_columns(5)
    token_columns(6)
    b_next(4)
    b_start(1)
    a_step(3, False)
    token_columns(7)
    give_back(1)
    b_next(-3)
    b_next(3)
    b_start(0)
    a_step(3, True)
    b_next(-2)
    b_y_end(4)
    b_next(2)
    a_step(4, False)
    b_next(-1)
    b_next(1)
    b_y_end(-3)
    b_y_end(3)
    pass_on(0)
    b_next(0)
    a_step(4, True)
    b_y_end(-2)
    b_y_end(2)
    b_y_end(-1)
    b_y_end(1)
    pass_on(1)
    a_z_end(2)
    a_z_end(-1)
    a_z_end(1)
    total_b = b_y_end(0)
    total_a = a_z_end(0)
    final[rows_a], final[rows_b] = total_a, total_b
    combine(0)
    b_end(final[rows_b])
    last = [to_other_core(rows_b, 0)]
    a_end(final[rows_a])
    last.append(to_other_core(rows_a, 1))
    combine(1)
    for copy in last:
        copy.wait_recv()
    store_shares()
    for copy in started:
        copy.wait_send()


def store_kernel(*refs):
    sources, targets, sems = refs[:3], refs[3:6], refs[6]
    stores = [pltpu.make_async_copy(sources[k], targets[k], sems.at[k]) for k in range(3)]
    for copy in stores:
        copy.start()
    for copy in stores:
        copy.wait()


def on_device(
    tokens, cotangent, expert_ids, gate_probs, gate_up_weight, down_weight, down_residual
):
    bf16, f32 = jnp.bfloat16, jnp.float32
    sems = pltpu.SemaphoreType.DMA
    vmem, anywhere = pl.BlockSpec(memory_space=pltpu.VMEM), pl.BlockSpec(memory_space=pl.ANY)
    shapes = (
        ((2, TOK), jnp.int32), ((2, TOK), f32),
        ((TOK, MODEL), bf16), ((TOK, MODEL), bf16), ((MODEL, WIDTH), bf16), ((UNITS, MODEL), bf16),
        ((UNITS, MODEL), bf16), ((WIDTH, MODEL), bf16), ((MODEL, UNITS), bf16),
        ((ROWS, TOK), bf16), ((TOK, ROWS), bf16), ((ROWS, TOK), f32), ((3 * CAP, MODEL), bf16), ((3 * CAP, MODEL), bf16),
        ((CAP, MODEL), bf16), ((CAP, MODEL), bf16),
        ((ROWS, MODEL), bf16), ((ROWS, MODEL), bf16), ((ROWS, WIDTH), f32), ((ROWS, WIDTH), bf16),
        ((ROWS, UNITS), bf16), ((MODEL, HALF), f32), ((UNITS, WIDTH), f32),
        *(2 * (((MODEL, 2 * CAP), bf16), ((MODEL, 2 * CAP), bf16), ((UNITS, 2 * CAP), bf16), ((UNITS, 2 * CAP), bf16))),
        ((ROWS, WIDTH), bf16), ((ROWS, HALF), bf16), ((UNITS, WIDTH), bf16),
        ((ROWS, MODEL), bf16), ((2, CAP, MODEL // 2), bf16), ((ROWS, MODEL), bf16),
        ((2 * CAP, UNITS), f32), ((CHIPS_Z, CHIPS_Y, SHARE, HALF), bf16),
        ((2, 4, CHIPS_Y, ROWS_A, HALF), bf16), ((3, ROWS_A, HALF), bf16),
        ((2, 2, CHIPS_Z, ROWS_B, HALF), bf16), ((2, 2, ROWS_B, HALF), bf16), ((4, ROWS_B, HALF), bf16),
        ((SHARE, HALF), f32), ((SHARE, HALF), f32),
    )
    semaphores = ((7,), (2, 12), (2, 2, 4), (2, 12), (2, 2, 4, 4), (2, 3), (2, 2, 2, 8), (2, 2, 2), (2, 7))
    results = (
        jax.ShapeDtypeStruct((TOK, MODEL), bf16),
        jax.ShapeDtypeStruct((GATE_ROWS, WIDTH), f32),
        jax.ShapeDtypeStruct((DOWN_ROWS, MODEL), f32),
    )
    values = pl.pallas_call(
        layer_kernel,
        out_shape=results,
        in_specs=[pl.BlockSpec(memory_space=pltpu.HBM)] * 7,
        out_specs=(vmem, vmem, vmem),
        scratch_shapes=[pltpu.VMEM(*shape) for shape in shapes] + [sems(shape) for shape in semaphores],
        compiler_params=pltpu.CompilerParams(
            collective_id=0, has_side_effects=True, vmem_limit_bytes=53 * 1024 * 1024
        ),
    )(
        expert_ids.T, gate_probs.T, tokens, cotangent, gate_up_weight[0], down_weight[0], down_residual[0, 0]
    )
    token_grad, gate_up_part, down_part = pl.pallas_call(
        store_kernel,
        out_shape=results,
        in_specs=[anywhere] * 3,
        out_specs=(anywhere,) * 3,
        scratch_shapes=[sems((3,))],
        compiler_params=pltpu.CompilerParams(vmem_limit_bytes=1024 * 1024),
    )(*values)
    return (token_grad, gate_up_part[None], down_part[None])


def solution(mesh):
    placed = (
        P(("dp", "expert"), None),
        P(("dp", "expert"), None),
        P(("dp", "expert"), None),
        P(("dp", "expert"), None),
        P("expert", None, None),
        P("expert", None, None),
        P("dp", "expert", None, None),
    )
    return jax.shard_map(
        on_device,
        mesh=mesh,
        in_specs=placed,
        out_specs=(P(("dp", "expert"), None), P("expert", "dp", None), P("expert", "dp", None)),
        check_vma=False,
    )
```

```python
import jax
import jax.numpy as jnp
from jax import lax
from jax.experimental import pallas as pl
from jax.experimental.pallas import tpu as pltpu
from jax.sharding import PartitionSpec as P

MESH = pl.DeviceIdType.MESH
CHIPS_Z, CHIPS_Y, CORES, EXPERTS = 8, 4, 2, 4
SHARE, WIDTH, HALF = 96, 1024, 512
GATE_ROWS, DOWN_ROWS = 32, 8
ROWS_A = 48
ROWS_B = SHARE - ROWS_A
FAR_PARTS = ((0, 32), (32, ROWS_B))
GROUPS = (4, -3, 3, -2, 2, -1, 1, 0)
ORDER_Y = (2, 1, -1, 0)
TOK, CAP, MODEL, UNITS = 128, 80, 2048, 512
ROWS = EXPERTS * CAP
OPP, SELF, LOW, HIGH = (slice(k * CAP, (k + 1) * CAP) for k in range(4))
EARLY, LATE, NEAR = slice(0, 2 * CAP), slice(2 * CAP, ROWS), slice(CAP, ROWS)


def wide(value):
    return value.astype(jnp.float32)


def dot(left, right):
    return jnp.dot(left, right, preferred_element_type=jnp.float32)


def dot_rows(left, right):
    return lax.dot_general(left, right, (((0,), (0,)), ((), ())), preferred_element_type=jnp.float32)


def columns(index, width):
    return pl.ds(pl.multiple_of(index * width, width), width)


def loop(count, body):
    def step(index, carry):
        body(index)
        return carry

    lax.fori_loop(0, count, step, 0)


def layer_kernel(
    ids_hbm, probs_hbm, tokens_hbm, cotangent_hbm, gate_up_hbm, down_hbm, residual_hbm,
    token_out, gate_out, down_out,
    ids_ref, probs_ref, tok_in, cot_in, gate_up, down, residual, gate_up_t, down_t,
    place, place_t, slot_weight, tok_send, grad_send, tok_relay, grad_relay,
    tok_all, grad_all, both, back, hidden, sum_gate, sum_down,
    tok_early, tok_late, hid_early, hid_late, tok_early_pair, tok_late_pair, hid_early_pair, hid_late_pair,
    grad_pair, back_pair, residual_pair,
    part, part_relay, returned,
    half_back, own, az_buf, ay_buf, by_buf, hub_buf, bz_buf, final, final_pair,
    load_sem, swap_sem, return_sem, pair_sem, az_sem, ay_sem, by_sem, hub_sem, bz_sem,
):
    bf16 = jnp.bfloat16
    me, x = lax.axis_index("dp"), lax.axis_index("expert")
    z, y, core = me // (CHIPS_Y * CORES), (me // CORES) % CHIPS_Y, me % CORES

    def at(zz, yy, cc):
        return (((zz + CHIPS_Z) % CHIPS_Z) * CHIPS_Y + (yy + CHIPS_Y) % CHIPS_Y) * CORES + cc

    def zi(off):
        return (z + off + CHIPS_Z) % CHIPS_Z

    def yi(off):
        return (y + off + CHIPS_Y) % CHIPS_Y

    partner = (at(z, y, 1 - core), x)
    z_side = ((at(z + 1, y, core), x), (at(z - 1, y, core), x))
    y_side = ((at(z, y + 1, core), x), (at(z, y - 1, core), x))
    x_side = ((me, (x + 1) % EXPERTS), (me, (x + EXPERTS - 1) % EXPERTS))
    barrier = pltpu.get_barrier_semaphore()
    z_far = [(at(z + off, y, core), x) for off in (2, -2)]
    y_far = [(at(z, y + 2, core), x)]
    for device in (partner, *z_side, *y_side, *x_side, *z_far, *y_far):
        pl.semaphore_signal(barrier, inc=1, device_id=device, device_id_type=MESH)

    loads = [
        pltpu.make_async_copy(source, target, load_sem.at[k])
        for k, (source, target) in enumerate(
            (
                (ids_hbm, ids_ref),
                (probs_hbm, probs_ref),
                (tokens_hbm, tok_in),
                (cotangent_hbm, cot_in),
                (down_hbm, down),
                (gate_up_hbm, gate_up),
                (residual_hbm, residual),
            )
        )
    ]
    for copy in loads:
        copy.start()

    started = []

    def send(src, dst, sems, index, device):
        copy = pltpu.make_async_remote_copy(
            src_ref=src, dst_ref=dst, send_sem=sems.at[(0, *index)], recv_sem=sems.at[(1, *index)],
            device_id=device, device_id_type=MESH,
        )
        copy.start()
        started.append(copy)
        return copy

    loads[0].wait()
    loads[1].wait()
    ids, probs = ids_ref[...], probs_ref[...]
    before = lax.broadcasted_iota(jnp.int32, (TOK, TOK), 0) < lax.broadcasted_iota(jnp.int32, (TOK, TOK), 1)
    before = jnp.where(before, 1.0, 0.0).astype(bf16)
    slots = wide(lax.broadcasted_iota(jnp.int32, (CAP, TOK), 0))
    for k in range(EXPERTS):
        expert = (x + k) % EXPERTS
        hits = ids == expert
        member = jnp.sum(jnp.where(hits, 1.0, 0.0), axis=0, keepdims=True)
        weight = jnp.sum(jnp.where(hits, probs, 0.0), axis=0, keepdims=True)
        index = dot(jnp.broadcast_to(member, (8, TOK)).astype(bf16), before)[0:1]
        chosen = jnp.where((slots == index) & (member > 0.5), 1.0, 0.0)
        rows = slice(k * CAP, (k + 1) * CAP)
        place[rows] = chosen.astype(bf16)
        slot_weight[rows] = jnp.broadcast_to(jnp.sum(chosen * weight, axis=1, keepdims=True), (CAP, TOK))

    def pick_tokens(k, target, rows):
        def body(n):
            cols = columns(n, 512)
            target[rows, cols] = dot(place[k * CAP : (k + 1) * CAP], tok_in[:, cols]).astype(bf16)
        loop(4, body)

    def pick_grads(k, target, rows):
        def body(n):
            cols = columns(n, 512)
            block = slice(k * CAP, (k + 1) * CAP)
            value = dot(place[block], cot_in[:, cols]) * slot_weight[block, 0:1]
            target[rows, cols] = value.astype(bf16)
        loop(4, body)

    swap = {}
    first, second, third = slice(0, CAP), slice(CAP, 2 * CAP), slice(2 * CAP, 3 * CAP)
    loads[2].wait()
    pick_tokens(2, tok_send, second)
    pl.semaphore_wait(barrier, 10)
    swap["tok", "leg"] = send(tok_send.at[second], tok_relay, swap_sem, (0,), x_side[0])
    loads[3].wait()
    pick_grads(2, grad_send, second)
    swap["grad", "leg"] = send(grad_send.at[second], grad_relay, swap_sem, (1,), x_side[1])
    pick_tokens(1, tok_send, first)
    left, right = slice(0, 1024), slice(1024, 2048)
    swap["tok", 0, 0] = send(tok_send.at[first, left], tok_all.at[LOW, left], swap_sem, (2,), x_side[0])
    pick_tokens(3, tok_send, third)
    swap["tok", 1, 0] = send(tok_send.at[third, left], tok_all.at[HIGH, left], swap_sem, (3,), x_side[1])
    pick_grads(1, grad_send, first)
    pick_grads(3, grad_send, third)
    pick_tokens(0, tok_all, SELF)
    pick_grads(0, grad_all, SELF)
    loads[4].wait()

    def turn_down(n):
        rows = columns(n, 256)
        down_t[rows, :] = down[:, rows].T

    loop(8, turn_down)
    swap["tok", "leg"].wait_recv()
    swap["tok", "far"] = send(tok_relay, tok_all.at[OPP], swap_sem, (4,), x_side[0])
    swap["grad", "leg"].wait_recv()
    swap["grad", "far"] = send(grad_relay, grad_all.at[OPP], swap_sem, (5,), x_side[1])
    swap["tok", 0, 1] = send(tok_send.at[first, right], tok_all.at[LOW, right], swap_sem, (10,), x_side[0])
    swap["tok", 1, 1] = send(tok_send.at[third, right], tok_all.at[HIGH, right], swap_sem, (11,), x_side[1])
    mine, theirs = columns(core, WIDTH), columns(1 - core, WIDTH)
    for part_at, cols in enumerate((theirs, mine)):
        swap["grad", 0, part_at] = send(
            grad_send.at[first, cols], grad_all.at[LOW, cols], swap_sem, (6 + part_at,), x_side[0]
        )
        swap["grad", 1, part_at] = send(
            grad_send.at[third, cols], grad_all.at[HIGH, cols], swap_sem, (8 + part_at,), x_side[1]
        )
    pair = {}

    def to_partner(name, index, src, dst):
        pair[name] = send(src, dst, pair_sem, (index,), partner)

    to_partner("grad self", 1, grad_all.at[SELF, theirs], grad_pair.at[SELF])
    loads[5].wait()

    def turn_gate_up(n):
        rows = columns(n, 256)
        gate_up_t[:, rows] = gate_up[rows, :].T

    loop(8, turn_gate_up)
    place_t[...] = place[...].T
    loads[6].wait()

    def project(rows):
        def body(n):
            cols = columns(n, 256)
            both[rows, cols] = dot(tok_all[rows], gate_up[:, cols])
        loop(4, body)

        def gates(n):
            r = pl.ds(pl.multiple_of(rows.start + n * 16, 16), 16)
            gate, up = both[r, 0:UNITS], both[r, UNITS : 2 * UNITS]
            sig = jax.nn.sigmoid(gate)
            active = gate * sig
            hidden[r] = (active * up).astype(bf16)
            both[r, 0:UNITS] = up * sig * (1.0 + gate * (1.0 - sig))
            both[r, UNITS : 2 * UNITS] = active
        loop((rows.stop - rows.start) // 16, gates)

    def pull_back(rows):
        def body(n):
            cols, upper = columns(n, 256), columns(n + 2, 256)
            value = dot(grad_all[rows], down_t[:, cols])
            back[rows, cols] = (value * both[rows, cols]).astype(bf16)
            back[rows, upper] = (value * both[rows, upper]).astype(bf16)
        loop(2, body)

    my_units, their_units = columns(core, HALF), columns(1 - core, HALF)
    to_partner("residual", 2, residual.at[:, theirs], residual_pair)
    def turn_tokens(rows, target):
        def body(n):
            cols = columns(n, 256)
            target[cols, :] = tok_all[rows, cols].T
        loop(8, body)

    def turn_hidden(rows, target):
        def body(n):
            cols = columns(n, 256)
            target[cols, :] = hidden[rows, cols].T
        loop(2, body)

    project(SELF)
    swap["tok", "far"].wait_recv()
    turn_tokens(EARLY, tok_early)
    to_partner("tok early", 4, tok_early, tok_early_pair)
    swap["grad", "far"].wait_recv()
    to_partner("grad far", 6, grad_all.at[OPP, theirs], grad_pair.at[OPP])
    project(OPP)
    turn_hidden(EARLY, hid_early)
    to_partner("hidden early", 5, hid_early, hid_early_pair)
    pull_back(EARLY)
    to_partner("back early", 7, back.at[EARLY, their_units], back_pair.at[EARLY])

    for part_at in range(2):
        for side in range(2):
            swap["tok", side, part_at].wait_recv()
    turn_tokens(LATE, tok_late)
    to_partner("tok late", 0, tok_late, tok_late_pair)
    project(LATE)
    turn_hidden(LATE, hid_late)
    to_partner("hidden late", 3, hid_late, hid_late_pair)
    def down_columns(half):
        return pl.ds(pl.multiple_of(core * WIDTH + half * 512, 512), 512)

    for name in ("residual", "grad self", "grad far", "hidden early"):
        pair[name].wait_recv()

    def early_down(n):
        rows = columns(n, 128)
        for half in range(2):
            cols = slice(half * 512, half * 512 + 512)
            start = wide(residual[rows, down_columns(half)]) + wide(residual_pair[rows, cols])
            start = start + dot(hid_early[rows], grad_all[EARLY, down_columns(half)])
            sum_down[rows, cols] = start + dot(hid_early_pair[rows], grad_pair[EARLY, cols])
    loop(4, early_down)
    for name in ("tok early", "back early"):
        pair[name].wait_recv()

    def early_gate(n):
        rows = columns(n, 256)
        value = dot(tok_early[rows], back[EARLY, my_units])
        sum_gate[rows, :] = value + dot(tok_early_pair[rows], back_pair[EARLY])
    loop(8, early_gate)

    swap["grad", 0, 0].wait_recv()
    to_partner("grad low", 9, grad_all.at[LOW, theirs], grad_pair.at[LOW])
    swap["grad", 1, 0].wait_recv()
    to_partner("grad high", 10, grad_all.at[HIGH, theirs], grad_pair.at[HIGH])

    def half_pull(n):
        cols = columns(n, 256)
        half_back[:, cols] = dot(grad_all[LATE, theirs], down_t[theirs, cols])
    loop(2, half_pull)
    swap["grad", 0, 1].wait_recv()
    swap["grad", 1, 1].wait_recv()

    def late_pull(n):
        cols, upper = columns(n, 256), columns(n + 2, 256)
        value = half_back[:, cols] + dot(grad_all[LATE, mine], down_t[mine, cols])
        back[LATE, cols] = (value * both[LATE, cols]).astype(bf16)
        back[LATE, upper] = (value * both[LATE, upper]).astype(bf16)
    loop(2, late_pull)
    to_partner("back late", 11, back.at[LATE, their_units], back_pair.at[LATE])
    for name in ("grad low", "grad high", "hidden late"):
        pair[name].wait_recv()

    def late_down(n):
        rows = columns(n, 128)
        for half in range(2):
            cols = slice(half * 512, half * 512 + 512)
            value = dot(hid_late[rows], grad_all[LATE, down_columns(half)])
            sum_down[rows, cols] += value + dot(hid_late_pair[rows], grad_pair[LATE, cols])
    loop(4, late_down)
    for name in ("tok late", "back late"):
        pair[name].wait_recv()

    def group(off):
        zz = zi(off)
        rows = columns(zz, 256)
        value = sum_gate[rows, :] + dot(tok_late[rows], back[LATE, my_units])
        value = value + dot(tok_late_pair[rows], back_pair[LATE])
        for yy in range(CHIPS_Y):
            down_rows = pl.ds(pl.multiple_of(zz * 64 + yy * 16, 16), 16)
            own[zz, yy, 0:64] = value[64 * yy : 64 * yy + 64].astype(bf16)
            own[zz, yy, 64:80] = sum_down[down_rows, 0:512].astype(bf16)
            own[zz, yy, 80:96] = sum_down[down_rows, 512:1024].astype(bf16)

    back_copies = {}

    def token_columns(n):
        cols = slice(n * 256, n * 256 + 256)
        value = dot(back[...], gate_up_t[:, cols]).astype(bf16)
        part[:, cols] = value
        returned[0:CAP, cols] = value[SELF]

    def give_back(half):
        cols = slice(half * 1024, half * 1024 + 1024)
        other = x_side[half]
        back_copies["leg", half] = send(
            part.at[OPP, cols], part_relay.at[half], return_sem, (half, 2), other
        )
        back_copies["high", half] = send(
            part.at[HIGH, cols], returned.at[3 * CAP : 4 * CAP, cols], return_sem, (half, 0), x_side[0]
        )
        back_copies["low", half] = send(
            part.at[LOW, cols], returned.at[CAP : 2 * CAP, cols], return_sem, (half, 1), x_side[1]
        )

    def pass_on(half):
        cols = slice(half * 1024, half * 1024 + 1024)
        back_copies["leg", half].wait_recv()
        back_copies["far", half] = send(
            part_relay.at[half], returned.at[2 * CAP : 3 * CAP, cols], return_sem, (half, 3), x_side[half]
        )

    def combine(half):
        for name in ("high", "low", "far"):
            back_copies[name, half].wait_recv()

        def body(n):
            cols = columns(n + 4 * half, 256)
            token_out[:, cols] = dot(place_t[...], returned[:, cols]).astype(bf16)
        loop(4, body)

    rows_a, rows_b = slice(0, ROWS_A), slice(ROWS_A, SHARE)
    copies = {}

    def add_into(zz, yy, rows, arrived):
        own[zz, yy, rows] = (wide(own[zz, yy, rows]) + wide(arrived)).astype(bf16)

    def a_z(side, step, off_y):
        off = (5 - step) if side == 0 else step - 5
        slot = ORDER_Y.index(off_y)
        if ("az", side, step - 1, off_y) in copies:
            copies["az", side, step - 1, off_y].wait_recv()
            add_into(zi(off), yi(off_y), rows_a, az_buf[side, step - 2, slot])
        copies["az", side, step, off_y] = send(
            own.at[zi(off), yi(off_y), rows_a], az_buf.at[side, step - 1, slot], az_sem,
            (side, step - 1, slot), z_side[side],
        )

    def a_z_end(off_y):
        slot = ORDER_Y.index(off_y)
        total = wide(own[z, yi(off_y), rows_a])
        for side in range(2):
            copies["az", side, 4, off_y].wait_recv()
            total = total + wide(az_buf[side, 3, slot])
        if off_y == 0:
            return total
        own[z, yi(off_y), rows_a] = total.astype(bf16)
        copies["ay", off_y] = send(
            own.at[z, yi(off_y), rows_a], ay_buf.at[slot], ay_sem, (slot,), (at(z, y + off_y, core), x)
        )

    def finish(total, rows):
        final[rows] = total * (1.0 / (CHIPS_Z * CHIPS_Y * CORES))

    def a_end(total):
        for off_y in (2, 1, -1):
            copies["ay", off_y].wait_recv()
            total = total + wide(ay_buf[ORDER_Y.index(off_y)])
        finish(total, rows_a)

    def b_y(side, step, piece):
        off = (3 - step) if side == 0 else step - 3
        slot = GROUPS.index(piece)
        if ("by", side, step - 1, piece) in copies:
            copies["by", side, step - 1, piece].wait_recv()
            add_into(zi(piece), yi(off), rows_b, by_buf[side, step - 2, slot])
        copies["by", side, step, piece] = send(
            own.at[zi(piece), yi(off), rows_b], by_buf.at[side, step - 1, slot], by_sem,
            (side, step - 1, slot), y_side[side],
        )

    def b_y_end(piece):
        slot = GROUPS.index(piece)
        total = wide(own[zi(piece), y, rows_b])
        for side in range(2):
            copies["by", side, 2, piece].wait_recv()
            total = total + wide(by_buf[side, 1, slot])
        if piece == 0:
            return total
        src = own.at[zi(piece), y]
        src[rows_b] = total.astype(bf16)
        if piece == 4:
            for side, (lo, hi) in enumerate(FAR_PARTS):
                copies["far", side] = send(
                    src.at[ROWS_A + lo : ROWS_A + hi], hub_buf.at[side, 0, lo:hi], hub_sem, (side, 0),
                    (at(z + (2, -2)[side], y, core), x),
                )
        elif abs(piece) == 3:
            side = 0 if piece > 0 else 1
            copies["near", side] = send(src.at[rows_b], hub_buf.at[side, 1], hub_sem, (side, 1), z_side[side])
        elif abs(piece) == 2:
            side = 0 if piece > 0 else 1
            lo, hi = FAR_PARTS[side]
            copies["far", side].wait_recv()
            copies["near", side].wait_recv()
            part_rows = slice(ROWS_A + lo, ROWS_A + hi)
            src[rows_b] = (wide(src[rows_b]) + wide(hub_buf[side, 1])).astype(bf16)
            src[part_rows] = (wide(src[part_rows]) + wide(hub_buf[side, 0, lo:hi])).astype(bf16)
            copies["bz", piece] = send(
                src.at[rows_b], bz_buf.at[side], bz_sem, (side,), (at(z + piece, y, core), x)
            )
        else:
            side = 0 if piece > 0 else 1
            copies["bz", piece] = send(src.at[rows_b], bz_buf.at[2 + side], bz_sem, (2 + side,), z_side[side])

    def b_end(total):
        for slot, piece in enumerate((2, -2, 1, -1)):
            copies["bz", piece].wait_recv()
            total = total + wide(bz_buf[slot])
        finish(total, rows_b)

    def to_other_core(rows, index):
        return send(final.at[rows], final_pair.at[rows], bz_sem, (4 + index,), partner)

    def store_shares():
        for source, units, first_col in ((final, my_units, core * WIDTH), (final_pair, their_units, (1 - core) * WIDTH)):
            gate_out[:, units] = source[pl.ds(pl.multiple_of(32 * core, 32), 32)]
            for k in range(2):
                cols = pl.ds(pl.multiple_of(first_col + k * 512, 512), 512)
                down_out[:, cols] = source[pl.ds(pl.multiple_of(64 + 16 * k + 8 * core, 8), 8)]

    upper = (4, 3, 2, 1)
    edge = {0: (2, 1), 1: (-1, 0)}

    def b_start(piece):
        far = 0 if piece in upper else 1
        b_y(far, 1, piece)
        b_y(1 - far, 2, piece)

    def b_next(piece):
        b_y(0 if piece in upper else 1, 2, piece)

    def a_step(step, own_edge):
        for k in range(2):
            for side in range(2):
                a_z(side, step, edge[side if own_edge else 1 - side][k])

    group(4)
    a_step(1, True)
    b_start(4)
    group(-3)
    for off_y in edge[0]:
        a_z(1, 2, off_y)
    group(3)
    for off_y in edge[1]:
        a_z(0, 2, off_y)
    b_start(-3)
    b_start(3)
    for off in GROUPS[3:]:
        group(off)
        if off in (-2, 2):
            b_start(off)
    for n in range(4):
        token_columns(n)
    give_back(0)
    token_columns(4)
    a_step(2, True)
    b_start(-1)
    token_columns(5)
    token_columns(6)
    b_next(4)
    b_start(1)
    a_step(3, False)
    token_columns(7)
    give_back(1)
    b_next(-3)
    b_next(3)
    b_start(0)
    a_step(3, True)
    b_next(-2)
    b_y_end(4)
    b_next(2)
    a_step(4, False)
    b_next(-1)
    b_next(1)
    b_y_end(-3)
    b_y_end(3)
    pass_on(0)
    b_next(0)
    a_step(4, True)
    b_y_end(-2)
    b_y_end(2)
    b_y_end(-1)
    b_y_end(1)
    pass_on(1)
    a_z_end(2)
    a_z_end(-1)
    a_z_end(1)
    total_b = b_y_end(0)
    total_a = a_z_end(0)
    final[rows_a], final[rows_b] = total_a, total_b
    combine(0)
    b_end(final[rows_b])
    last = [to_other_core(rows_b, 0)]
    a_end(final[rows_a])
    last.append(to_other_core(rows_a, 1))
    combine(1)
    for copy in last:
        copy.wait_recv()
    store_shares()
    for copy in started:
        copy.wait_send()


def store_kernel(*refs):
    sources, targets, sems = refs[:3], refs[3:6], refs[6]
    stores = [pltpu.make_async_copy(sources[k], targets[k], sems.at[k]) for k in range(3)]
    for copy in stores:
        copy.start()
    for copy in stores:
        copy.wait()


def on_device(
    tokens, cotangent, expert_ids, gate_probs, gate_up_weight, down_weight, down_residual
):
    bf16, f32 = jnp.bfloat16, jnp.float32
    sems = pltpu.SemaphoreType.DMA
    vmem, anywhere = pl.BlockSpec(memory_space=pltpu.VMEM), pl.BlockSpec(memory_space=pl.ANY)
    shapes = (
        ((2, TOK), jnp.int32), ((2, TOK), f32),
        ((TOK, MODEL), bf16), ((TOK, MODEL), bf16), ((MODEL, WIDTH), bf16), ((UNITS, MODEL), bf16),
        ((UNITS, MODEL), bf16), ((WIDTH, MODEL), bf16), ((MODEL, UNITS), bf16),
        ((ROWS, TOK), bf16), ((TOK, ROWS), bf16), ((ROWS, TOK), f32), ((3 * CAP, MODEL), bf16), ((3 * CAP, MODEL), bf16),
        ((CAP, MODEL), bf16), ((CAP, MODEL), bf16),
        ((ROWS, MODEL), bf16), ((ROWS, MODEL), bf16), ((ROWS, WIDTH), f32), ((ROWS, WIDTH), bf16),
        ((ROWS, UNITS), bf16), ((MODEL, HALF), f32), ((UNITS, WIDTH), f32),
        *(2 * (((MODEL, 2 * CAP), bf16), ((MODEL, 2 * CAP), bf16), ((UNITS, 2 * CAP), bf16), ((UNITS, 2 * CAP), bf16))),
        ((ROWS, WIDTH), bf16), ((ROWS, HALF), bf16), ((UNITS, WIDTH), bf16),
        ((ROWS, MODEL), bf16), ((2, CAP, MODEL // 2), bf16), ((ROWS, MODEL), bf16),
        ((2 * CAP, UNITS), f32), ((CHIPS_Z, CHIPS_Y, SHARE, HALF), bf16),
        ((2, 4, CHIPS_Y, ROWS_A, HALF), bf16), ((3, ROWS_A, HALF), bf16),
        ((2, 2, CHIPS_Z, ROWS_B, HALF), bf16), ((2, 2, ROWS_B, HALF), bf16), ((4, ROWS_B, HALF), bf16),
        ((SHARE, HALF), f32), ((SHARE, HALF), f32),
    )
    semaphores = ((7,), (2, 12), (2, 2, 4), (2, 12), (2, 2, 4, 4), (2, 3), (2, 2, 2, 8), (2, 2, 2), (2, 7))
    results = (
        jax.ShapeDtypeStruct((TOK, MODEL), bf16),
        jax.ShapeDtypeStruct((GATE_ROWS, WIDTH), f32),
        jax.ShapeDtypeStruct((DOWN_ROWS, MODEL), f32),
    )
    values = pl.pallas_call(
        layer_kernel,
        out_shape=results,
        in_specs=[pl.BlockSpec(memory_space=pltpu.HBM)] * 7,
        out_specs=(vmem, vmem, vmem),
        scratch_shapes=[pltpu.VMEM(*shape) for shape in shapes] + [sems(shape) for shape in semaphores],
        compiler_params=pltpu.CompilerParams(
            collective_id=0, has_side_effects=True, vmem_limit_bytes=53 * 1024 * 1024
        ),
    )(
        expert_ids.T, gate_probs.T, tokens, cotangent, gate_up_weight[0], down_weight[0], down_residual[0, 0]
    )
    token_grad, gate_up_part, down_part = pl.pallas_call(
        store_kernel,
        out_shape=results,
        in_specs=[anywhere] * 3,
        out_specs=(anywhere,) * 3,
        scratch_shapes=[sems((3,))],
        compiler_params=pltpu.CompilerParams(vmem_limit_bytes=1024 * 1024),
    )(*values)
    return (token_grad, gate_up_part[None], down_part[None])


def solution(mesh):
    placed = (
        P(("dp", "expert"), None),
        P(("dp", "expert"), None),
        P(("dp", "expert"), None),
        P(("dp", "expert"), None),
        P("expert", None, None),
        P("expert", None, None),
        P("dp", "expert", None, None),
    )
    return jax.shard_map(
        on_device,
        mesh=mesh,
        in_specs=placed,
        out_specs=(P(("dp", "expert"), None), P("expert", "dp", None), P("expert", "dp", None)),
        check_vma=False,
    )
```

```python
import jax
import jax.numpy as jnp
from jax import lax
from jax.experimental import pallas as pl
from jax.experimental.pallas import tpu as pltpu
from jax.sharding import PartitionSpec as P

MESH = pl.DeviceIdType.MESH
CHIPS_Z, CHIPS_Y, CORES, EXPERTS = 8, 4, 2, 4
SHARE, WIDTH, HALF = 96, 1024, 512
GATE_ROWS, DOWN_ROWS = 32, 8
ROWS_A = 48
ROWS_B = SHARE - ROWS_A
FAR_PARTS = ((0, 32), (32, ROWS_B))
GROUPS = (4, -3, 3, -2, 2, -1, 1, 0)
ORDER_Y = (2, 1, -1, 0)
TOK, CAP, MODEL, UNITS = 128, 80, 2048, 512
ROWS = EXPERTS * CAP
OPP, SELF, LOW, HIGH = (slice(k * CAP, (k + 1) * CAP) for k in range(4))
EARLY, LATE, NEAR = slice(0, 2 * CAP), slice(2 * CAP, ROWS), slice(CAP, ROWS)


def wide(value):
    return value.astype(jnp.float32)


def dot(left, right):
    return jnp.dot(left, right, preferred_element_type=jnp.float32)


def dot_rows(left, right):
    return lax.dot_general(left, right, (((0,), (0,)), ((), ())), preferred_element_type=jnp.float32)


def columns(index, width):
    return pl.ds(pl.multiple_of(index * width, width), width)


def loop(count, body):
    def step(index, carry):
        body(index)
        return carry

    lax.fori_loop(0, count, step, 0)


def layer_kernel(
    ids_hbm, probs_hbm, tokens_hbm, cotangent_hbm, gate_up_hbm, down_hbm, residual_hbm,
    token_out, gate_out, down_out,
    ids_ref, probs_ref, tok_in, cot_in, gate_up, down, residual, gate_up_t, down_t,
    place, place_t, slot_weight, tok_send, grad_send, tok_relay, grad_relay,
    tok_all, grad_all, both, back, hidden, sum_gate, sum_down,
    tok_early, tok_late, hid_early, hid_late, tok_early_pair, tok_late_pair, hid_early_pair, hid_late_pair,
    grad_pair, back_pair, residual_pair,
    part, part_relay, returned,
    half_back, own, az_buf, ay_buf, by_buf, hub_buf, bz_buf, final, final_pair,
    load_sem, swap_sem, return_sem, pair_sem, az_sem, ay_sem, by_sem, hub_sem, bz_sem,
):
    bf16 = jnp.bfloat16
    me, x = lax.axis_index("dp"), lax.axis_index("expert")
    z, y, core = me // (CHIPS_Y * CORES), (me // CORES) % CHIPS_Y, me % CORES

    def at(zz, yy, cc):
        return (((zz + CHIPS_Z) % CHIPS_Z) * CHIPS_Y + (yy + CHIPS_Y) % CHIPS_Y) * CORES + cc

    def zi(off):
        return (z + off + CHIPS_Z) % CHIPS_Z

    def yi(off):
        return (y + off + CHIPS_Y) % CHIPS_Y

    partner = (at(z, y, 1 - core), x)
    z_side = ((at(z + 1, y, core), x), (at(z - 1, y, core), x))
    y_side = ((at(z, y + 1, core), x), (at(z, y - 1, core), x))
    x_side = ((me, (x + 1) % EXPERTS), (me, (x + EXPERTS - 1) % EXPERTS))
    barrier = pltpu.get_barrier_semaphore()
    z_far = [(at(z + off, y, core), x) for off in (2, -2)]
    y_far = [(at(z, y + 2, core), x)]
    for device in (partner, *z_side, *y_side, *x_side, *z_far, *y_far):
        pl.semaphore_signal(barrier, inc=1, device_id=device, device_id_type=MESH)

    loads = [
        pltpu.make_async_copy(source, target, load_sem.at[k])
        for k, (source, target) in enumerate(
            (
                (ids_hbm, ids_ref),
                (probs_hbm, probs_ref),
                (tokens_hbm, tok_in),
                (cotangent_hbm, cot_in),
                (down_hbm, down),
                (gate_up_hbm, gate_up),
                (residual_hbm, residual),
            )
        )
    ]
    for copy in loads:
        copy.start()

    started = []

    def send(src, dst, sems, index, device):
        copy = pltpu.make_async_remote_copy(
            src_ref=src, dst_ref=dst, send_sem=sems.at[(0, *index)], recv_sem=sems.at[(1, *index)],
            device_id=device, device_id_type=MESH,
        )
        copy.start()
        started.append(copy)
        return copy

    loads[0].wait()
    loads[1].wait()
    ids, probs = ids_ref[...], probs_ref[...]
    before = lax.broadcasted_iota(jnp.int32, (TOK, TOK), 0) < lax.broadcasted_iota(jnp.int32, (TOK, TOK), 1)
    before = jnp.where(before, 1.0, 0.0).astype(bf16)
    slots = wide(lax.broadcasted_iota(jnp.int32, (CAP, TOK), 0))
    for k in range(EXPERTS):
        expert = (x + k) % EXPERTS
        hits = ids == expert
        member = jnp.sum(jnp.where(hits, 1.0, 0.0), axis=0, keepdims=True)
        weight = jnp.sum(jnp.where(hits, probs, 0.0), axis=0, keepdims=True)
        index = dot(jnp.broadcast_to(member, (8, TOK)).astype(bf16), before)[0:1]
        chosen = jnp.where((slots == index) & (member > 0.5), 1.0, 0.0)
        rows = slice(k * CAP, (k + 1) * CAP)
        place[rows] = chosen.astype(bf16)
        slot_weight[rows] = jnp.broadcast_to(jnp.sum(chosen * weight, axis=1, keepdims=True), (CAP, TOK))

    def pick_tokens(k, target, rows):
        def body(n):
            cols = columns(n, 512)
            target[rows, cols] = dot(place[k * CAP : (k + 1) * CAP], tok_in[:, cols]).astype(bf16)
        loop(4, body)

    def pick_grads(k, target, rows):
        def body(n):
            cols = columns(n, 512)
            block = slice(k * CAP, (k + 1) * CAP)
            value = dot(place[block], cot_in[:, cols]) * slot_weight[block, 0:1]
            target[rows, cols] = value.astype(bf16)
        loop(4, body)

    swap = {}
    first, second, third = slice(0, CAP), slice(CAP, 2 * CAP), slice(2 * CAP, 3 * CAP)
    loads[2].wait()
    pick_tokens(2, tok_send, second)
    pl.semaphore_wait(barrier, 10)
    swap["tok", "leg"] = send(tok_send.at[second], tok_relay, swap_sem, (0,), x_side[0])
    loads[3].wait()
    pick_grads(2, grad_send, second)
    swap["grad", "leg"] = send(grad_send.at[second], grad_relay, swap_sem, (1,), x_side[1])
    pick_tokens(1, tok_send, first)
    left, right = slice(0, 1024), slice(1024, 2048)
    swap["tok", 0, 0] = send(tok_send.at[first, left], tok_all.at[LOW, left], swap_sem, (2,), x_side[0])
    pick_tokens(3, tok_send, third)
    swap["tok", 1, 0] = send(tok_send.at[third, left], tok_all.at[HIGH, left], swap_sem, (3,), x_side[1])
    pick_grads(1, grad_send, first)
    pick_grads(3, grad_send, third)
    pick_tokens(0, tok_all, SELF)
    pick_grads(0, grad_all, SELF)
    loads[4].wait()

    def turn_down(n):
        rows = columns(n, 256)
        down_t[rows, :] = down[:, rows].T

    loop(8, turn_down)
    swap["tok", "leg"].wait_recv()
    swap["tok", "far"] = send(tok_relay, tok_all.at[OPP], swap_sem, (4,), x_side[0])
    swap["grad", "leg"].wait_recv()
    swap["grad", "far"] = send(grad_relay, grad_all.at[OPP], swap_sem, (5,), x_side[1])
    swap["tok", 0, 1] = send(tok_send.at[first, right], tok_all.at[LOW, right], swap_sem, (10,), x_side[0])
    swap["tok", 1, 1] = send(tok_send.at[third, right], tok_all.at[HIGH, right], swap_sem, (11,), x_side[1])
    mine, theirs = columns(core, WIDTH), columns(1 - core, WIDTH)
    for part_at, cols in enumerate((theirs, mine)):
        swap["grad", 0, part_at] = send(
            grad_send.at[first, cols], grad_all.at[LOW, cols], swap_sem, (6 + part_at,), x_side[0]
        )
        swap["grad", 1, part_at] = send(
            grad_send.at[third, cols], grad_all.at[HIGH, cols], swap_sem, (8 + part_at,), x_side[1]
        )
    pair = {}

    def to_partner(name, index, src, dst):
        pair[name] = send(src, dst, pair_sem, (index,), partner)

    to_partner("grad self", 1, grad_all.at[SELF, theirs], grad_pair.at[SELF])
    loads[5].wait()

    def turn_gate_up(n):
        rows = columns(n, 256)
        gate_up_t[:, rows] = gate_up[rows, :].T

    loop(8, turn_gate_up)
    place_t[...] = place[...].T
    loads[6].wait()

    def project(rows):
        def body(n):
            cols = columns(n, 256)
            both[rows, cols] = dot(tok_all[rows], gate_up[:, cols])
        loop(4, body)

        def gates(n):
            r = pl.ds(pl.multiple_of(rows.start + n * 16, 16), 16)
            gate, up = both[r, 0:UNITS], both[r, UNITS : 2 * UNITS]
            sig = jax.nn.sigmoid(gate)
            active = gate * sig
            hidden[r] = (active * up).astype(bf16)
            both[r, 0:UNITS] = up * sig * (1.0 + gate * (1.0 - sig))
            both[r, UNITS : 2 * UNITS] = active
        loop((rows.stop - rows.start) // 16, gates)

    def pull_back(rows):
        def body(n):
            cols, upper = columns(n, 256), columns(n + 2, 256)
            value = dot(grad_all[rows], down_t[:, cols])
            back[rows, cols] = (value * both[rows, cols]).astype(bf16)
            back[rows, upper] = (value * both[rows, upper]).astype(bf16)
        loop(2, body)

    my_units, their_units = columns(core, HALF), columns(1 - core, HALF)
    to_partner("residual", 2, residual.at[:, theirs], residual_pair)
    def turn_tokens(rows, target):
        def body(n):
            cols = columns(n, 256)
            target[cols, :] = tok_all[rows, cols].T
        loop(8, body)

    def turn_hidden(rows, target):
        def body(n):
            cols = columns(n, 256)
            target[cols, :] = hidden[rows, cols].T
        loop(2, body)

    project(SELF)
    swap["tok", "far"].wait_recv()
    turn_tokens(EARLY, tok_early)
    to_partner("tok early", 4, tok_early, tok_early_pair)
    swap["grad", "far"].wait_recv()
    to_partner("grad far", 6, grad_all.at[OPP, theirs], grad_pair.at[OPP])
    project(OPP)
    turn_hidden(EARLY, hid_early)
    to_partner("hidden early", 5, hid_early, hid_early_pair)
    pull_back(EARLY)
    to_partner("back early", 7, back.at[EARLY, their_units], back_pair.at[EARLY])

    for part_at in range(2):
        for side in range(2):
            swap["tok", side, part_at].wait_recv()
    turn_tokens(LATE, tok_late)
    to_partner("tok late", 0, tok_late, tok_late_pair)
    project(LATE)
    turn_hidden(LATE, hid_late)
    to_partner("hidden late", 3, hid_late, hid_late_pair)
    def down_columns(half):
        return pl.ds(pl.multiple_of(core * WIDTH + half * 512, 512), 512)

    for name in ("residual", "grad self", "grad far", "hidden early"):
        pair[name].wait_recv()

    def early_down(n):
        rows = columns(n, 128)
        for half in range(2):
            cols = slice(half * 512, half * 512 + 512)
            start = wide(residual[rows, down_columns(half)]) + wide(residual_pair[rows, cols])
            start = start + dot(hid_early[rows], grad_all[EARLY, down_columns(half)])
            sum_down[rows, cols] = start + dot(hid_early_pair[rows], grad_pair[EARLY, cols])
    loop(4, early_down)
    for name in ("tok early", "back early"):
        pair[name].wait_recv()

    swap["grad", 0, 0].wait_recv()
    to_partner("grad low", 9, grad_all.at[LOW, theirs], grad_pair.at[LOW])
    swap["grad", 1, 0].wait_recv()
    to_partner("grad high", 10, grad_all.at[HIGH, theirs], grad_pair.at[HIGH])

    def half_pull(n):
        cols = columns(n, 256)
        half_back[:, cols] = dot(grad_all[LATE, theirs], down_t[theirs, cols])
    loop(2, half_pull)
    swap["grad", 0, 1].wait_recv()
    swap["grad", 1, 1].wait_recv()

    def late_pull(n):
        cols, upper = columns(n, 256), columns(n + 2, 256)
        value = half_back[:, cols] + dot(grad_all[LATE, mine], down_t[mine, cols])
        back[LATE, cols] = (value * both[LATE, cols]).astype(bf16)
        back[LATE, upper] = (value * both[LATE, upper]).astype(bf16)
    loop(2, late_pull)
    to_partner("back late", 11, back.at[LATE, their_units], back_pair.at[LATE])
    for name in ("grad low", "grad high", "hidden late"):
        pair[name].wait_recv()

    def late_down(n):
        rows = columns(n, 128)
        for half in range(2):
            cols = slice(half * 512, half * 512 + 512)
            value = dot(hid_late[rows], grad_all[LATE, down_columns(half)])
            sum_down[rows, cols] += value + dot(hid_late_pair[rows], grad_pair[LATE, cols])
    loop(4, late_down)
    for name in ("tok late", "back late"):
        pair[name].wait_recv()

    def group(off):
        zz = zi(off)
        rows = columns(zz, 256)
        value = dot(tok_early[rows], back[EARLY, my_units])
        value = value + dot(tok_early_pair[rows], back_pair[EARLY])
        value = value + dot(tok_late[rows], back[LATE, my_units])
        value = value + dot(tok_late_pair[rows], back_pair[LATE])
        for yy in range(CHIPS_Y):
            down_rows = pl.ds(pl.multiple_of(zz * 64 + yy * 16, 16), 16)
            own[zz, yy, 0:64] = value[64 * yy : 64 * yy + 64].astype(bf16)
            own[zz, yy, 64:80] = sum_down[down_rows, 0:512].astype(bf16)
            own[zz, yy, 80:96] = sum_down[down_rows, 512:1024].astype(bf16)

    back_copies = {}

    def token_columns(n):
        cols = slice(n * 256, n * 256 + 256)
        value = dot(back[...], gate_up_t[:, cols]).astype(bf16)
        part[:, cols] = value
        returned[0:CAP, cols] = value[SELF]

    def give_back(half):
        cols = slice(half * 1024, half * 1024 + 1024)
        other = x_side[half]
        back_copies["leg", half] = send(
            part.at[OPP, cols], part_relay.at[half], return_sem, (half, 2), other
        )
        back_copies["high", half] = send(
            part.at[HIGH, cols], returned.at[3 * CAP : 4 * CAP, cols], return_sem, (half, 0), x_side[0]
        )
        back_copies["low", half] = send(
            part.at[LOW, cols], returned.at[CAP : 2 * CAP, cols], return_sem, (half, 1), x_side[1]
        )

    def pass_on(half):
        cols = slice(half * 1024, half * 1024 + 1024)
        back_copies["leg", half].wait_recv()
        back_copies["far", half] = send(
            part_relay.at[half], returned.at[2 * CAP : 3 * CAP, cols], return_sem, (half, 3), x_side[half]
        )

    def combine(half):
        for name in ("high", "low", "far"):
            back_copies[name, half].wait_recv()

        def body(n):
            cols = columns(n + 4 * half, 256)
            token_out[:, cols] = dot(place_t[...], returned[:, cols]).astype(bf16)
        loop(4, body)

    rows_a, rows_b = slice(0, ROWS_A), slice(ROWS_A, SHARE)
    copies = {}

    def add_into(zz, yy, rows, arrived):
        own[zz, yy, rows] = (wide(own[zz, yy, rows]) + wide(arrived)).astype(bf16)

    def a_z(side, step, off_y):
        off = (5 - step) if side == 0 else step - 5
        slot = ORDER_Y.index(off_y)
        if ("az", side, step - 1, off_y) in copies:
            copies["az", side, step - 1, off_y].wait_recv()
            add_into(zi(off), yi(off_y), rows_a, az_buf[side, step - 2, slot])
        copies["az", side, step, off_y] = send(
            own.at[zi(off), yi(off_y), rows_a], az_buf.at[side, step - 1, slot], az_sem,
            (side, step - 1, slot), z_side[side],
        )

    def a_z_end(off_y):
        slot = ORDER_Y.index(off_y)
        total = wide(own[z, yi(off_y), rows_a])
        for side in range(2):
            copies["az", side, 4, off_y].wait_recv()
            total = total + wide(az_buf[side, 3, slot])
        if off_y == 0:
            return total
        own[z, yi(off_y), rows_a] = total.astype(bf16)
        copies["ay", off_y] = send(
            own.at[z, yi(off_y), rows_a], ay_buf.at[slot], ay_sem, (slot,), (at(z, y + off_y, core), x)
        )

    def finish(total, rows):
        final[rows] = total * (1.0 / (CHIPS_Z * CHIPS_Y * CORES))

    def a_end(total):
        for off_y in (2, 1, -1):
            copies["ay", off_y].wait_recv()
            total = total + wide(ay_buf[ORDER_Y.index(off_y)])
        finish(total, rows_a)

    def b_y(side, step, piece):
        off = (3 - step) if side == 0 else step - 3
        slot = GROUPS.index(piece)
        if ("by", side, step - 1, piece) in copies:
            copies["by", side, step - 1, piece].wait_recv()
            add_into(zi(piece), yi(off), rows_b, by_buf[side, step - 2, slot])
        copies["by", side, step, piece] = send(
            own.at[zi(piece), yi(off), rows_b], by_buf.at[side, step - 1, slot], by_sem,
            (side, step - 1, slot), y_side[side],
        )

    def b_y_end(piece):
        slot = GROUPS.index(piece)
        total = wide(own[zi(piece), y, rows_b])
        for side in range(2):
            copies["by", side, 2, piece].wait_recv()
            total = total + wide(by_buf[side, 1, slot])
        if piece == 0:
            return total
        src = own.at[zi(piece), y]
        src[rows_b] = total.astype(bf16)
        if piece == 4:
            for side, (lo, hi) in enumerate(FAR_PARTS):
                copies["far", side] = send(
                    src.at[ROWS_A + lo : ROWS_A + hi], hub_buf.at[side, 0, lo:hi], hub_sem, (side, 0),
                    (at(z + (2, -2)[side], y, core), x),
                )
        elif abs(piece) == 3:
            side = 0 if piece > 0 else 1
            copies["near", side] = send(src.at[rows_b], hub_buf.at[side, 1], hub_sem, (side, 1), z_side[side])
        elif abs(piece) == 2:
            side = 0 if piece > 0 else 1
            lo, hi = FAR_PARTS[side]
            copies["far", side].wait_recv()
            copies["near", side].wait_recv()
            part_rows = slice(ROWS_A + lo, ROWS_A + hi)
            src[rows_b] = (wide(src[rows_b]) + wide(hub_buf[side, 1])).astype(bf16)
            src[part_rows] = (wide(src[part_rows]) + wide(hub_buf[side, 0, lo:hi])).astype(bf16)
            copies["bz", piece] = send(
                src.at[rows_b], bz_buf.at[side], bz_sem, (side,), (at(z + piece, y, core), x)
            )
        else:
            side = 0 if piece > 0 else 1
            copies["bz", piece] = send(src.at[rows_b], bz_buf.at[2 + side], bz_sem, (2 + side,), z_side[side])

    def b_end(total):
        for slot, piece in enumerate((2, -2, 1, -1)):
            copies["bz", piece].wait_recv()
            total = total + wide(bz_buf[slot])
        finish(total, rows_b)

    def to_other_core(rows, index):
        return send(final.at[rows], final_pair.at[rows], bz_sem, (4 + index,), partner)

    def store_shares():
        for source, units, first_col in ((final, my_units, core * WIDTH), (final_pair, their_units, (1 - core) * WIDTH)):
            gate_out[:, units] = source[pl.ds(pl.multiple_of(32 * core, 32), 32)]
            for k in range(2):
                cols = pl.ds(pl.multiple_of(first_col + k * 512, 512), 512)
                down_out[:, cols] = source[pl.ds(pl.multiple_of(64 + 16 * k + 8 * core, 8), 8)]

    upper = (4, 3, 2, 1)
    edge = {0: (2, 1), 1: (-1, 0)}

    def b_start(piece):
        far = 0 if piece in upper else 1
        b_y(far, 1, piece)
        b_y(1 - far, 2, piece)

    def b_next(piece):
        b_y(0 if piece in upper else 1, 2, piece)

    def a_step(step, own_edge):
        for k in range(2):
            for side in range(2):
                a_z(side, step, edge[side if own_edge else 1 - side][k])

    group(4)
    a_step(1, True)
    b_start(4)
    group(-3)
    for off_y in edge[0]:
        a_z(1, 2, off_y)
    group(3)
    for off_y in edge[1]:
        a_z(0, 2, off_y)
    b_start(-3)
    b_start(3)
    for off in GROUPS[3:]:
        group(off)
        if off in (-2, 2):
            b_start(off)
    for n in range(4):
        token_columns(n)
    give_back(0)
    token_columns(4)
    a_step(2, True)
    b_start(-1)
    token_columns(5)
    token_columns(6)
    b_next(4)
    b_start(1)
    a_step(3, False)
    token_columns(7)
    give_back(1)
    b_next(-3)
    b_next(3)
    b_start(0)
    a_step(3, True)
    b_next(-2)
    b_y_end(4)
    b_next(2)
    a_step(4, False)
    b_next(-1)
    b_next(1)
    b_y_end(-3)
    b_y_end(3)
    pass_on(0)
    b_next(0)
    a_step(4, True)
    b_y_end(-2)
    b_y_end(2)
    b_y_end(-1)
    b_y_end(1)
    pass_on(1)
    a_z_end(2)
    a_z_end(-1)
    a_z_end(1)
    total_b = b_y_end(0)
    total_a = a_z_end(0)
    final[rows_a], final[rows_b] = total_a, total_b
    combine(0)
    b_end(final[rows_b])
    last = [to_other_core(rows_b, 0)]
    a_end(final[rows_a])
    last.append(to_other_core(rows_a, 1))
    combine(1)
    for copy in last:
        copy.wait_recv()
    store_shares()
    for copy in started:
        copy.wait_send()


def store_kernel(*refs):
    sources, targets, sems = refs[:3], refs[3:6], refs[6]
    stores = [pltpu.make_async_copy(sources[k], targets[k], sems.at[k]) for k in range(3)]
    for copy in stores:
        copy.start()
    for copy in stores:
        copy.wait()


def on_device(
    tokens, cotangent, expert_ids, gate_probs, gate_up_weight, down_weight, down_residual
):
    bf16, f32 = jnp.bfloat16, jnp.float32
    sems = pltpu.SemaphoreType.DMA
    vmem, anywhere = pl.BlockSpec(memory_space=pltpu.VMEM), pl.BlockSpec(memory_space=pl.ANY)
    shapes = (
        ((2, TOK), jnp.int32), ((2, TOK), f32),
        ((TOK, MODEL), bf16), ((TOK, MODEL), bf16), ((MODEL, WIDTH), bf16), ((UNITS, MODEL), bf16),
        ((UNITS, MODEL), bf16), ((WIDTH, MODEL), bf16), ((MODEL, UNITS), bf16),
        ((ROWS, TOK), bf16), ((TOK, ROWS), bf16), ((ROWS, TOK), f32), ((3 * CAP, MODEL), bf16), ((3 * CAP, MODEL), bf16),
        ((CAP, MODEL), bf16), ((CAP, MODEL), bf16),
        ((ROWS, MODEL), bf16), ((ROWS, MODEL), bf16), ((ROWS, WIDTH), f32), ((ROWS, WIDTH), bf16),
        ((ROWS, UNITS), bf16), ((MODEL, HALF), f32), ((UNITS, WIDTH), f32),
        *(2 * (((MODEL, 2 * CAP), bf16), ((MODEL, 2 * CAP), bf16), ((UNITS, 2 * CAP), bf16), ((UNITS, 2 * CAP), bf16))),
        ((ROWS, WIDTH), bf16), ((ROWS, HALF), bf16), ((UNITS, WIDTH), bf16),
        ((ROWS, MODEL), bf16), ((2, CAP, MODEL // 2), bf16), ((ROWS, MODEL), bf16),
        ((2 * CAP, UNITS), f32), ((CHIPS_Z, CHIPS_Y, SHARE, HALF), bf16),
        ((2, 4, CHIPS_Y, ROWS_A, HALF), bf16), ((3, ROWS_A, HALF), bf16),
        ((2, 2, CHIPS_Z, ROWS_B, HALF), bf16), ((2, 2, ROWS_B, HALF), bf16), ((4, ROWS_B, HALF), bf16),
        ((SHARE, HALF), f32), ((SHARE, HALF), f32),
    )
    semaphores = ((7,), (2, 12), (2, 2, 4), (2, 12), (2, 2, 4, 4), (2, 3), (2, 2, 2, 8), (2, 2, 2), (2, 7))
    results = (
        jax.ShapeDtypeStruct((TOK, MODEL), bf16),
        jax.ShapeDtypeStruct((GATE_ROWS, WIDTH), f32),
        jax.ShapeDtypeStruct((DOWN_ROWS, MODEL), f32),
    )
    values = pl.pallas_call(
        layer_kernel,
        out_shape=results,
        in_specs=[pl.BlockSpec(memory_space=pltpu.HBM)] * 7,
        out_specs=(vmem, vmem, vmem),
        scratch_shapes=[pltpu.VMEM(*shape) for shape in shapes] + [sems(shape) for shape in semaphores],
        compiler_params=pltpu.CompilerParams(
            collective_id=0, has_side_effects=True, vmem_limit_bytes=53 * 1024 * 1024
        ),
    )(
        expert_ids.T, gate_probs.T, tokens, cotangent, gate_up_weight[0], down_weight[0], down_residual[0, 0]
    )
    token_grad, gate_up_part, down_part = pl.pallas_call(
        store_kernel,
        out_shape=results,
        in_specs=[anywhere] * 3,
        out_specs=(anywhere,) * 3,
        scratch_shapes=[sems((3,))],
        compiler_params=pltpu.CompilerParams(vmem_limit_bytes=1024 * 1024),
    )(*values)
    return (token_grad, gate_up_part[None], down_part[None])


def solution(mesh):
    placed = (
        P(("dp", "expert"), None),
        P(("dp", "expert"), None),
        P(("dp", "expert"), None),
        P(("dp", "expert"), None),
        P("expert", None, None),
        P("expert", None, None),
        P("dp", "expert", None, None),
    )
    return jax.shard_map(
        on_device,
        mesh=mesh,
        in_specs=placed,
        out_specs=(P(("dp", "expert"), None), P("expert", "dp", None), P("expert", "dp", None)),
        check_vma=False,
    )
```
